32 devices in a mesh: vocab: 16 (over z, y, core), tok: 2 (over x).
Axes of the slice: x: 2, y: 2, z: 4, core: 2. Of those that a mesh axis runs over, the one named last changes fastest.
Arguments:
- hidden: bfloat16 [256, 3584], P('tok', 'vocab'), may hold values from -8 to 8
- head_weight: bfloat16 [3584, 81920], P('tok', 'vocab'), may hold values from -4 to 4
- targets: int32 [256], P('tok'), may hold values from 0 to 81919
- response_mask: int32 [256], P('tok'), may hold values 0 or 1
- labels: int32 [2], P('tok'), may hold values 0 or 1
- reference_sums: float32 [2, 2], P('tok'), may hold values from -48 to 48
Outputs:
- mean_loss: float32 [], replicated
- margins: float32 [2], P('tok')
- hidden_grad: bfloat16 [256, 3584], P('tok', 'vocab')
- head_grad: bfloat16 [3584, 81920], P('tok', 'vocab')
The draws below stay inside these ranges and needn't reach their ends.
All inputs are finite; a program needn't handle non-finite values. No bound on the sum of `response_mask` or of `labels` on one device may be relied on, other than what follows from the above.
Results may differ from the reference program's by a relative error of at most 0.0085.
Values may be sent and summed in bfloat16 or wider, within the bound.
No kernel may reach another device: no remote copies, remote signals or barrier semaphores. Data moves between devices by JAX's collectives and lax.ppermute only.
A program may use at most 128 MiB of HBM per device.

```python
import math
import jax
import jax.numpy as jnp
import numpy as np

D = 3584
VOCAB = 81920
RESP_LEN = 64
PAIRS = 2
TOKENS = 256


group_width = 32


topic_weight = 6.0


def joint_draw(key):
    key_head = jax.random.fold_in(key, 101)
    key_scale = jax.random.fold_in(key, 102)
    key_rows = jax.random.fold_in(key, 103)
    key_topic = jax.random.fold_in(key, 107)
    key_boost = jax.random.fold_in(key, 108)
    key_jitter = jax.random.fold_in(key, 109)
    key_dirs = jax.random.fold_in(key, 110)
    group_count = VOCAB // group_width
    pair_count = TOKENS // (2 * RESP_LEN)
    directions = jnp.clip(jax.random.normal(key_dirs, (group_count, D), jnp.float32), -6.0, 6.0) / math.sqrt(D)
    col_scale = jnp.exp(jax.random.uniform(key_scale, (1, VOCAB), jnp.float32, math.log(0.3), math.log(3.0)))
    head = jnp.clip(jax.random.normal(key_head, (D, VOCAB), jnp.float32), -6.0, 6.0) * (12.0 / math.sqrt(D)) * col_scale
    head = head.reshape(D, group_count, group_width) + topic_weight * directions.T[:, :, None]
    head = jnp.clip(head.reshape(D, VOCAB), -4.0, 4.0)
    noise_rows = jnp.clip(jax.random.normal(key_rows, (TOKENS, D), jnp.float32), -6.0, 6.0) * 0.06
    pair_topic = jax.random.randint(key_topic, (pair_count,), 0, group_count)
    pair_boost = math.log(VOCAB / group_width) + jax.random.uniform(key_boost, (pair_count,), jnp.float32, -1.5, 2.5)
    row_topic = jnp.repeat(pair_topic, 2 * RESP_LEN)
    row_boost = jnp.repeat(pair_boost, 2 * RESP_LEN) + jax.random.uniform(key_jitter, (TOKENS,), jnp.float32, -0.5, 0.5)
    row_dirs = jnp.take(directions, row_topic, axis=0)
    rows = noise_rows + (row_boost / topic_weight)[:, None] * row_dirs
    rows = jnp.clip(rows, -8.0, 8.0)
    return (rows, head)


def draw_hidden(key, part):
    return joint_draw(key)[0].astype(jnp.bfloat16)


def draw_head_weight(key, part):
    return joint_draw(key)[1].astype(jnp.bfloat16)


def with_ends(result, own_key, least, high):
    longest = result.shape.index(max(result.shape))
    spots = []
    for shift in (0, 1):
        where = [jax.random.randint(jax.random.fold_in(own_key, axis), (), 0, length) for axis, length in enumerate(result.shape)]
        where[longest] = (where[longest] + shift) % result.shape[longest]
        spots.append(tuple(where))
    return result.at[spots[0]].set(least).at[spots[1]].set(high)


def shard_levels(key, extent, cuts, smallest, high):
    factor_of, own = 1.0, jax.random.fold_in(key, 6)
    for dim, parts in cuts:
        draws = jnp.exp(jax.random.uniform(jax.random.fold_in(own, dim), (parts,), jnp.float32, smallest / len(cuts), high / len(cuts)))
        factor_of = factor_of * jnp.repeat(draws, extent[dim] // parts).reshape([-1 if axis == dim else 1 for axis in range(len(extent))])
    return factor_of


def ranked_wide(key, extent, number_of, skew):
    portions = [min(1 << octave, number_of + 1 - (1 << octave)) * (1 << 20) // math.isqrt((1 << octave) ** skew) + 1 for octave in range((number_of + 1).bit_length()) if 1 << octave <= number_of]
    width = 1 + sum(portions) // (1 << 30)
    listing = np.cumsum(np.array([max(1, weight // width) for weight in portions]))
    lot = jax.random.randint(jax.random.fold_in(key, 1), extent, 0, int(listing[len(portions) - 1]))
    start = jnp.left_shift(1, jnp.searchsorted(jnp.asarray(listing, jnp.int32), lot, side="right").astype(jnp.int32))
    rank = start - 1 + jax.random.randint(jax.random.fold_in(key, 4), extent, 0, 1 << 30) % jnp.minimum(start, number_of + 1 - start)
    return jax.random.permutation(jax.random.fold_in(key, 2), number_of)[rank].astype(jnp.int32)


def gaussian(own_key, extent, deviation, most, shards=(), kind=jnp.bfloat16):
    values = deviation * jax.random.normal(own_key, extent, jnp.float32)
    if shards:
        values = values * shard_levels(own_key, extent, shards, -0.22, 0.18)
    return jnp.clip(values, -most, most).astype(kind)


def setup_inputs(seed: int = 0) -> dict:
    key_list = jax.random.split(jax.random.key(seed), 7)
    return {
        "hidden": draw_hidden(jax.random.fold_in(key_list[6], 71), 0),
        "head_weight": draw_head_weight(jax.random.fold_in(key_list[6], 71), 0),
        "targets": with_ends(ranked_wide(key_list[2], (TOKENS,), VOCAB, 2), jax.random.fold_in(key_list[2], 3), 0, VOCAB - 1).astype(jnp.int32),
        "response_mask": with_ends((jax.random.randint(key_list[3], (TOKENS,), 0, 8) < 7).astype(jnp.int32), jax.random.fold_in(key_list[3], 1), 0, 1),
        "labels": with_ends((jax.random.randint(key_list[4], (PAIRS,), 0, 2) < 1).astype(jnp.int32), jax.random.fold_in(key_list[4], 1), 0, 1),
        "reference_sums": gaussian(key_list[5], (PAIRS, 2), 8.0, 48.0, ((0, 2),), jnp.float32),
    }


beta_scale = 0.1
tie_offset = math.log(2.0)
tie_const = math.log(3.0)
grad_scale = 512.0


def pair_terms(margins, labels):
    winner = labels.astype(jnp.float32)
    log_tie = tie_const + margins - tie_offset - jax.nn.softplus(margins - tie_offset) - jax.nn.softplus(margins + tie_offset)
    losses = winner * jax.nn.softplus(tie_offset - margins) - (1.0 - winner) * log_tie
    slopes = -winner * jax.nn.sigmoid(tie_offset - margins) - (1.0 - winner) * (1.0 - jax.nn.sigmoid(margins - tie_offset) - jax.nn.sigmoid(margins + tie_offset))
    return losses, slopes


def reference(hidden, head_weight, targets, response_mask, labels, reference_sums):
    logits = jnp.dot(hidden, head_weight, preferred_element_type=jnp.float32)
    row_max = jnp.max(logits, axis=1, keepdims=True)
    shifted = jnp.exp(logits - row_max)
    totals = jnp.sum(shifted, axis=1)
    target_logit = jnp.take_along_axis(logits, targets.astype(jnp.int32)[:, None], axis=1)[:, 0]
    token_logp = target_logit - (row_max[:, 0] + jnp.log(totals))
    weights = response_mask.astype(jnp.float32)
    sequence_logp = jnp.sum((token_logp * weights).reshape(PAIRS, 2, RESP_LEN), axis=2)
    ratios = sequence_logp - reference_sums
    margins = beta_scale * (ratios[:, 0] - ratios[:, 1])
    losses, slopes = pair_terms(margins, labels)
    mean_loss = jnp.sum(losses) / PAIRS
    pair_coef = (beta_scale * grad_scale / PAIRS) * slopes
    signed = jnp.stack([pair_coef, -pair_coef], axis=1)
    token_coef = jnp.broadcast_to(signed[:, :, None], (PAIRS, 2, RESP_LEN)).reshape(TOKENS) * weights
    columns = jnp.arange(VOCAB, dtype=jnp.int32)
    onehot = jnp.where(columns[None, :] == targets.astype(jnp.int32)[:, None], 1.0, 0.0).astype(jnp.float32)
    probs = shifted / totals[:, None]
    dlogits = (token_coef[:, None] * (onehot - probs)).astype(jnp.bfloat16)
    hidden_grad = jnp.dot(dlogits, head_weight.T, preferred_element_type=jnp.float32).astype(jnp.bfloat16)
    head_grad = jnp.dot(hidden.T, dlogits, preferred_element_type=jnp.float32).astype(jnp.bfloat16)
    return (mean_loss, margins, hidden_grad, head_grad)
```

```python
import math

import jax
import jax.numpy as jnp
from jax import lax
from jax.sharding import PartitionSpec as P

beta_scale = 0.1
tie_offset = math.log(2.0)
tie_const = math.log(3.0)
grad_scale = 512.0


def pair_terms(margins, labels):
    winner = labels.astype(jnp.float32)
    log_tie = (
        tie_const
        + margins
        - tie_offset
        - jax.nn.softplus(margins - tie_offset)
        - jax.nn.softplus(margins + tie_offset)
    )
    losses = winner * jax.nn.softplus(tie_offset - margins) - (1.0 - winner) * log_tie
    slopes = -winner * jax.nn.sigmoid(tie_offset - margins) - (1.0 - winner) * (
        1.0 - jax.nn.sigmoid(margins - tie_offset) - jax.nn.sigmoid(margins + tie_offset)
    )
    return (losses, slopes)


def add_parts(received):
    return jnp.sum(received, axis=0)


def general_local(hidden, head_weight, targets, response_mask, labels, reference_sums):
    tok_rows = hidden.shape[0]
    vocab_cols = head_weight.shape[1]
    tok_count = lax.axis_size("tok")
    pair_local = labels.shape[0]
    pair_total = pair_local * tok_count
    span = tok_rows // (2 * pair_local)
    rows_full = lax.all_gather(hidden, "vocab", axis=1, tiled=True)
    token_cols = lax.all_to_all(rows_full, "tok", split_axis=1, concat_axis=0, tiled=True)
    partial_value = jnp.dot(token_cols, head_weight, preferred_element_type=jnp.float32)
    partial_value = partial_value.reshape(tok_count, tok_rows, vocab_cols)
    logits = add_parts(
        lax.all_to_all(partial_value, "tok", split_axis=0, concat_axis=0, tiled=True)
    )
    offset = lax.axis_index("vocab") * vocab_cols
    columns = lax.broadcasted_iota(jnp.int32, (1, vocab_cols), 1) + offset
    matched = columns == targets[:, None]
    local_max = jnp.max(logits, axis=1)
    local_target = jnp.sum(jnp.where(matched, logits, 0.0), axis=1)
    row_max = lax.pmax(local_max, "vocab")
    shifted = jnp.exp(logits - row_max[:, None])
    totals, target_logit = lax.psum((jnp.sum(shifted, axis=1), local_target), "vocab")
    probs = shifted / totals[:, None]
    token_logp = target_logit - (row_max + jnp.log(totals))
    weights = response_mask.astype(jnp.float32)
    sequence_logp = jnp.sum((token_logp * weights).reshape(pair_local, 2, span), axis=2)
    ratios = sequence_logp - reference_sums
    margins = beta_scale * (ratios[:, 0] - ratios[:, 1])
    losses, slopes = pair_terms(margins, labels)
    mean_loss = lax.psum(jnp.sum(losses), "tok") / pair_total
    pair_coef = beta_scale * grad_scale / pair_total * slopes
    signed = jnp.stack([pair_coef, -pair_coef], axis=1)
    token_coef = (
        jnp.broadcast_to(signed[:, :, None], (pair_local, 2, span)).reshape(tok_rows) * weights
    )
    onehot = jnp.where(matched, 1.0, 0.0).astype(jnp.float32)
    dlogits = (token_coef[:, None] * (onehot - probs)).astype(jnp.bfloat16)
    dlogit_all = lax.all_gather(dlogits, "tok", axis=0, tiled=True)
    head_grad = lax.dot_general(
        token_cols, dlogit_all, (((0,), (0,)), ((), ())), preferred_element_type=jnp.float32
    ).astype(jnp.bfloat16)
    partial_grad = lax.dot_general(
        head_weight, dlogit_all, (((1,), (1,)), ((), ())), preferred_element_type=jnp.float32
    )
    returned = lax.all_to_all(
        partial_grad.astype(jnp.bfloat16), "tok", split_axis=1, concat_axis=0, tiled=True
    ).astype(partial_grad.dtype)
    grad_cols = lax.psum_scatter(returned, "vocab", scatter_dimension=0, tiled=True)
    hidden_grad = grad_cols.T.astype(jnp.bfloat16)
    return (mean_loss, margins, hidden_grad, head_grad)


swap_pairs = ((0, 1), (1, 0))
hidden_bound = 8.0
weight_bound = 4.0
half_limit = 60000.0


def exclusive(count, mask):
    return [(spot, spot ^ mask) for spot in range(count)]


def by_bit(bit, own, other, axis):
    low = jnp.where(bit == 0, own, other)
    high = jnp.where(bit == 0, other, own)
    return jnp.concatenate([low, high], axis=axis)


def merge_stats(bit, own, other):
    first = jnp.where(bit == 0, own, other)
    second = jnp.where(bit == 0, other, own)
    top = jnp.maximum(first[0], second[0])
    total = first[1] * jnp.exp(first[0] - top) + second[1] * jnp.exp(second[0] - top)
    return jnp.stack([top, total, first[2] + second[2]])


def gather_stats(stats, spot, count):
    mask = 1
    while mask < count:
        bit = (spot // mask) % 2
        if 2 * mask < count:
            near = lax.ppermute(stats, "vocab", exclusive(count, mask))
            far = lax.ppermute(stats, "vocab", exclusive(count, 2 * mask))
            both = lax.ppermute(stats, "vocab", exclusive(count, 3 * mask))
            one = merge_stats(bit, stats, near)
            two = merge_stats(bit, far, both)
            stats = merge_stats((spot // (2 * mask)) % 2, one, two)
            mask *= 4
        else:
            near = lax.ppermute(stats, "vocab", exclusive(count, mask))
            stats = merge_stats(bit, stats, near)
            mask *= 2
    return stats


def plane_swap(value, count, moves):
    half = count // 2
    pairs = []
    for plane in range(2):
        for spot in range(count):
            if spot // half != plane:
                pairs.append((2 * spot + plane, 2 * (spot ^ half) + 1 - plane))
    received = lax.ppermute(value, ("vocab", "tok"), pairs)
    return jnp.where(moves, received, value)


def scatter_sum(partial, spot, count):
    mask = 1
    value = partial
    while mask < count:
        bit = (spot // mask) % 2
        value = value.reshape((-1, 2) + partial.shape[1:])
        send = jnp.where(bit == 0, value[:, 1], value[:, 0]).astype(jnp.bfloat16)
        keep = jnp.where(bit == 0, value[:, 0], value[:, 1])
        value = keep + lax.ppermute(send, "vocab", exclusive(count, mask)).astype(jnp.float32)
        mask *= 2
    return value.reshape(partial.shape[1:])


def paired_local(hidden, head_weight, targets, response_mask, labels, reference_sums):
    rows = hidden.shape[0]
    feats = hidden.shape[1]
    depth, cols = head_weight.shape
    pair_local = labels.shape[0]
    pair_total = 2 * pair_local
    span = rows // (2 * pair_local)
    count = lax.axis_size("vocab")
    half = count // 2
    plane = lax.axis_index("tok")
    spot = lax.axis_index("vocab")
    moves = spot // half != plane

    def both_planes(value):
        return by_bit(plane, value, lax.ppermute(value, "tok", swap_pairs), 0)

    targets_all = both_planes(targets)
    weights_all = both_planes(response_mask.astype(jnp.float32))
    labels_all = both_planes(labels)
    refs_all = both_planes(reference_sums)

    piece = plane_swap(hidden.T, count, moves)
    pieces = lax.all_gather(piece, "vocab", axis=0, tiled=True)
    hidden_t = pieces.reshape(2, depth, rows).transpose(1, 0, 2).reshape(depth, 2 * rows)
    hidden_n = hidden_t.T

    scale = 1.0
    while hidden_bound * weight_bound * depth * scale > half_limit:
        scale *= 0.5
    parts = 5 if cols % (5 * 128) == 0 else 1
    width = cols // parts
    logit_parts = []
    for part in range(parts):
        block = lax.slice_in_dim(head_weight, part * width, (part + 1) * width, axis=1)
        own = jnp.dot(hidden_n, block, preferred_element_type=jnp.float32)
        sent = (own * scale if scale != 1.0 else own).astype(jnp.float16)
        got = lax.ppermute(sent, "tok", swap_pairs).astype(jnp.float32)
        logit_parts.append(own + (got * (1.0 / scale) if scale != 1.0 else got))
    logits = jnp.concatenate(logit_parts, axis=1)
    offset = spot * cols
    columns = lax.broadcasted_iota(jnp.int32, (1, cols), 1) + offset
    matched = columns == targets_all[:, None]
    local_max = jnp.max(logits, axis=1)
    local_sum = jnp.sum(jnp.exp(logits - local_max[:, None]), axis=1)
    local_target = jnp.sum(jnp.where(matched, logits, 0.0), axis=1)
    row_max, totals, target_logit = gather_stats(
        jnp.stack([local_max, local_sum, local_target]), spot, count
    )
    token_logp = target_logit - (row_max + jnp.log(totals))
    sequence_logp = jnp.sum((token_logp * weights_all).reshape(pair_total, 2, span), axis=2)
    ratios = sequence_logp - refs_all
    margins_all = beta_scale * (ratios[:, 0] - ratios[:, 1])
    losses, slopes = pair_terms(margins_all, labels_all)
    margins = jnp.where(plane == 0, margins_all[:pair_local], margins_all[pair_local:])
    own_loss = jnp.where(plane == 0, jnp.sum(losses[:pair_local]), jnp.sum(losses[pair_local:]))
    mean_loss = (own_loss + lax.ppermute(own_loss, "tok", swap_pairs)) / pair_total
    pair_coef = beta_scale * grad_scale / pair_total * slopes
    signed = jnp.stack([pair_coef, -pair_coef], axis=1)
    token_coef = (
        jnp.broadcast_to(signed[:, :, None], (pair_total, 2, span)).reshape(2 * rows) * weights_all
    )
    onehot = jnp.where(matched, 1.0, 0.0).astype(jnp.float32)
    probs = jnp.exp(logits - row_max[:, None]) / totals[:, None]
    dlogits = (token_coef[:, None] * (onehot - probs)).astype(jnp.bfloat16)
    partial = lax.dot_general(
        head_weight, dlogits, (((1,), (1,)), ((), ())), preferred_element_type=jnp.float32
    )
    partial = partial.reshape(half, feats, 2, rows).transpose(2, 0, 1, 3)
    summed = scatter_sum(partial.reshape(count, feats, rows), spot, count)
    hidden_grad = plane_swap(summed.astype(jnp.bfloat16), count, moves).T
    head_grad = jnp.dot(hidden_t, dlogits, preferred_element_type=jnp.float32).astype(
        jnp.bfloat16
    )
    return (mean_loss, margins, hidden_grad, head_grad)


def solution(mesh):
    count = mesh.shape["vocab"]
    paired = mesh.shape["tok"] == 2 and count >= 2 and count & (count - 1) == 0
    return jax.shard_map(
        paired_local if paired else general_local,
        mesh=mesh,
        in_specs=(
            P("tok", "vocab"),
            P("tok", "vocab"),
            P("tok"),
            P("tok"),
            P("tok"),
            P("tok", None),
        ),
        out_specs=(P(), P("tok"), P("tok", "vocab"), P("tok", "vocab")),
        check_vma=False,
    )
```

```python
import functools
import math

import jax
import jax.numpy as jnp
from jax import lax
from jax.experimental import pallas as pl
from jax.experimental.pallas import tpu as pltpu
from jax.sharding import PartitionSpec as P


beta_scale = 0.1
tie_offset = math.log(2.0)
tie_const = math.log(3.0)
grad_scale = 512.0


def pair_terms(margins, labels):
    winner = labels.astype(jnp.float32)
    log_tie = (
        tie_const
        + margins
        - tie_offset
        - jax.nn.softplus(margins - tie_offset)
        - jax.nn.softplus(margins + tie_offset)
    )
    losses = winner * jax.nn.softplus(tie_offset - margins) - (1.0 - winner) * log_tie
    slopes = -winner * jax.nn.sigmoid(tie_offset - margins) - (1.0 - winner) * (
        1.0 - jax.nn.sigmoid(margins - tie_offset) - jax.nn.sigmoid(margins + tie_offset)
    )
    return (losses, slopes)


def add_parts(received):
    return jnp.sum(received, axis=0)


def general_local(hidden, head_weight, targets, response_mask, labels, reference_sums):
    tok_rows = hidden.shape[0]
    vocab_cols = head_weight.shape[1]
    tok_count = lax.axis_size("tok")
    pair_local = labels.shape[0]
    pair_total = pair_local * tok_count
    span = tok_rows // (2 * pair_local)
    rows_full = lax.all_gather(hidden, "vocab", axis=1, tiled=True)
    token_cols = lax.all_to_all(rows_full, "tok", split_axis=1, concat_axis=0, tiled=True)
    partial_value = jnp.dot(token_cols, head_weight, preferred_element_type=jnp.float32)
    partial_value = partial_value.reshape(tok_count, tok_rows, vocab_cols)
    logits = add_parts(
        lax.all_to_all(partial_value, "tok", split_axis=0, concat_axis=0, tiled=True)
    )
    offset = lax.axis_index("vocab") * vocab_cols
    columns = lax.broadcasted_iota(jnp.int32, (1, vocab_cols), 1) + offset
    matched = columns == targets[:, None]
    local_max = jnp.max(logits, axis=1)
    local_target = jnp.sum(jnp.where(matched, logits, 0.0), axis=1)
    row_max = lax.pmax(local_max, "vocab")
    shifted = jnp.exp(logits - row_max[:, None])
    totals, target_logit = lax.psum((jnp.sum(shifted, axis=1), local_target), "vocab")
    probs = shifted / totals[:, None]
    token_logp = target_logit - (row_max + jnp.log(totals))
    weights = response_mask.astype(jnp.float32)
    sequence_logp = jnp.sum((token_logp * weights).reshape(pair_local, 2, span), axis=2)
    ratios = sequence_logp - reference_sums
    margins = beta_scale * (ratios[:, 0] - ratios[:, 1])
    losses, slopes = pair_terms(margins, labels)
    mean_loss = lax.psum(jnp.sum(losses), "tok") / pair_total
    pair_coef = beta_scale * grad_scale / pair_total * slopes
    signed = jnp.stack([pair_coef, -pair_coef], axis=1)
    token_coef = (
        jnp.broadcast_to(signed[:, :, None], (pair_local, 2, span)).reshape(tok_rows) * weights
    )
    onehot = jnp.where(matched, 1.0, 0.0).astype(jnp.float32)
    dlogits = (token_coef[:, None] * (onehot - probs)).astype(jnp.bfloat16)
    dlogit_all = lax.all_gather(dlogits, "tok", axis=0, tiled=True)
    head_grad = lax.dot_general(
        token_cols, dlogit_all, (((0,), (0,)), ((), ())), preferred_element_type=jnp.float32
    ).astype(jnp.bfloat16)
    partial_grad = lax.dot_general(
        head_weight, dlogit_all, (((1,), (1,)), ((), ())), preferred_element_type=jnp.float32
    )
    returned = lax.all_to_all(
        partial_grad.astype(jnp.bfloat16), "tok", split_axis=1, concat_axis=0, tiled=True
    ).astype(partial_grad.dtype)
    grad_cols = lax.psum_scatter(returned, "vocab", scatter_dimension=0, tiled=True)
    hidden_grad = grad_cols.T.astype(jnp.bfloat16)
    return (mean_loss, margins, hidden_grad, head_grad)


swap_pairs = ((0, 1), (1, 0))
hidden_bound = 8.0
weight_bound = 4.0
half_limit = 60000.0
part_tiles = (4, 4, 8, 8, 8, 4, 4)
mebi = 1 << 20


def exclusive(count, mask):
    return [(spot, spot ^ mask) for spot in range(count)]


def across(value, count, mask):
    return lax.ppermute(value, "vocab", exclusive(count, mask))


def over(value):
    return lax.ppermute(value, "tok", swap_pairs)


def plane_swap(value, count, moves):
    half = count // 2
    pairs = []
    for plane in range(2):
        for spot in range(count):
            if spot // half != plane:
                pairs.append((2 * spot + plane, 2 * (spot ^ half) + 1 - plane))
    received = lax.ppermute(value, ("vocab", "tok"), pairs)
    return jnp.where(moves, received, value)


def place_kernel(order, spot_ref, *refs):
    hidden_t_ref, hidden_n_ref = refs[-2:]
    slots, feats, rows = refs[0].shape
    half = 2 * slots
    spot = spot_ref[0]
    for side, ref in zip((0, 2, 1, 3), refs[:-2]):
        for slot in range(slots):
            source = spot ^ (order[slot] ^ side)
            start = pl.multiple_of((source % half) * feats, 32)
            column = pl.multiple_of((source // half) * rows, 128)
            hidden_t_ref[pl.ds(start, feats), pl.ds(column, rows)] = ref[slot]
    depth = hidden_t_ref.shape[0]
    step = 256 if depth % 256 == 0 else 128
    for start in range(0, depth, step):
        hidden_n_ref[:, start : start + step] = hidden_t_ref[start : start + step, :].T


def fold_kernel(start, has_state, logits_ref, target_ref, weight_ref, *refs):
    if has_state:
        stats_ref, grad_ref, new_stats_ref, new_grad_ref, terms_ref = refs
    else:
        new_stats_ref, new_grad_ref, terms_ref = refs
    logits = logits_ref[...]
    width = logits.shape[1]
    columns = lax.broadcasted_iota(jnp.int32, logits.shape, 1) + start
    hit = columns == target_ref[...]
    top = jnp.max(logits, axis=1, keepdims=True)
    if has_state:
        old = stats_ref[...].T
        old_top = old[:, 0:1]
        top = jnp.maximum(top, old_top)
    terms = jnp.exp(logits - top)
    total = jnp.sum(terms, axis=1, keepdims=True)
    target = jnp.sum(jnp.where(hit, logits, 0.0), axis=1, keepdims=True)
    terms_ref[...] = jnp.where(hit, 0.0, terms).astype(jnp.bfloat16)
    shrink = jnp.ones_like(top)
    if has_state:
        shrink = jnp.exp(old_top - top)
        total = total + old[:, 1:2] * shrink
        target = target + old[:, 2:3]
    lane = lax.broadcasted_iota(jnp.int32, (logits.shape[0], 128), 1)
    packed = jnp.where(
        lane == 0, top, jnp.where(lane == 1, total, jnp.where(lane == 2, target, shrink))
    ).T
    new_stats_ref[...] = packed[0:8]
    shrink_row = packed[3:4]
    depth = weight_ref.shape[0]
    step = depth // 2 if depth % 256 == 0 else depth
    for first in range(0, depth, step):
        part = lax.dot_general(
            weight_ref[first : first + step, start : start + width],
            terms_ref[...],
            (((1,), (1,)), ((), ())),
            preferred_element_type=jnp.float32,
        )
        if has_state:
            part = part + grad_ref[first : first + step, :] * shrink_row
        new_grad_ref[first : first + step, :] = part


def fold(start, width, logits, local_targets, head_weight, state):
    tokens = logits.shape[0]
    depth = head_weight.shape[0]
    args = [logits, local_targets, head_weight]
    aliases = {}
    if state is not None:
        args += list(state)
        aliases = {4: 1}
    return pl.pallas_call(
        functools.partial(fold_kernel, start, state is not None),
        out_shape=(
            jax.ShapeDtypeStruct((8, tokens), jnp.float32),
            jax.ShapeDtypeStruct((depth, tokens), jnp.float32),
        ),
        in_specs=vmem_specs(len(args)),
        out_specs=tuple(vmem_specs(2)),
        scratch_shapes=[pltpu.VMEM((tokens, width), jnp.bfloat16)],
        input_output_aliases=aliases,
        compiler_params=pltpu.CompilerParams(vmem_limit_bytes=12 * mebi),
        cost_estimate=pl.CostEstimate(
            flops=2 * depth * tokens * width,
            transcendentals=tokens * width,
            bytes_accessed=2 * depth * width + 4 * tokens * width + 8 * depth * tokens,
        ),
    )(*args)


def load_kernel(source_ref, held_ref, sems):
    number = sems.shape[0]
    rows = source_ref.shape[0] // number
    copies = [
        pltpu.make_async_copy(
            source_ref.at[pl.ds(index * rows, rows)],
            held_ref.at[pl.ds(index * rows, rows)],
            sems.at[index],
        )
        for index in range(number)
    ]
    for copy in copies:
        copy.start()
    for copy in copies:
        copy.wait()


def load(head_weight):
    depth = head_weight.shape[0]
    number = 8 if depth % 256 == 0 else 1
    return pl.pallas_call(
        load_kernel,
        out_shape=pltpu.VMEM(head_weight.shape, head_weight.dtype),
        in_specs=[pl.BlockSpec(memory_space=pl.ANY)],
        out_specs=pl.BlockSpec(memory_space=pltpu.VMEM),
        scratch_shapes=[pltpu.SemaphoreType.DMA((number,))],
        compiler_params=pltpu.CompilerParams(vmem_limit_bytes=20 * mebi),
        cost_estimate=pl.CostEstimate(
            flops=0, transcendentals=0, bytes_accessed=2 * head_weight.size
        ),
    )(head_weight)


def logit_kernel(start, hidden_ref, weight_ref, out_ref):
    width = out_ref.shape[1]
    step = 256 if width % 256 == 0 else width
    for first in range(0, width, step):
        out_ref[:, first : first + step] = jnp.dot(
            hidden_ref[...],
            weight_ref[:, start + first : start + first + step],
            preferred_element_type=jnp.float32,
        )


def logit_part(start, width, hidden_n, head_weight):
    tokens, depth = hidden_n.shape
    return pl.pallas_call(
        functools.partial(logit_kernel, start),
        out_shape=jax.ShapeDtypeStruct((tokens, width), jnp.float32),
        in_specs=vmem_specs(2),
        out_specs=vmem_specs(1)[0],
        compiler_params=pltpu.CompilerParams(vmem_limit_bytes=12 * mebi),
        cost_estimate=pl.CostEstimate(
            flops=2 * depth * tokens * width, transcendentals=0, bytes_accessed=2 * depth * width
        ),
    )(hidden_n, head_weight)


def gather_hidden(piece, where, count):
    order = [0]
    parts = [piece]
    for mask in range(4, count, 4):
        order.append(mask)
        parts.append(across(piece, count, mask))
    feats, rows = piece.shape
    stacked = jnp.concatenate(parts, axis=0)
    side = across(stacked, count, 2)
    groups = [stacked, side, across(stacked, count, 1), across(side, count, 1)]
    slots = len(order)
    depth = 2 * slots * feats
    return pl.pallas_call(
        lambda *refs: place_kernel(order, *refs),
        out_shape=(
            jax.ShapeDtypeStruct((depth, 2 * rows), piece.dtype),
            jax.ShapeDtypeStruct((2 * rows, depth), piece.dtype),
        ),
        in_specs=[pl.BlockSpec(memory_space=pltpu.SMEM)]
        + [pl.BlockSpec(memory_space=pltpu.VMEM)] * len(groups),
        out_specs=[pl.BlockSpec(memory_space=pltpu.VMEM)] * 2,
        compiler_params=pltpu.CompilerParams(vmem_limit_bytes=8 * mebi),
        cost_estimate=pl.CostEstimate(flops=0, transcendentals=0, bytes_accessed=4000000),
    )(
        where,
        *[group.reshape(slots, feats, rows) for group in groups],
    )


def pick_kernel(feats, spot_ref, target_ref, weight_ref, keep_ref, send_ref, sum_ref):
    _, cols = weight_ref.shape
    width = 1024 if cols % 1024 == 0 else cols
    columns = lax.broadcasted_iota(jnp.int32, (target_ref.shape[0], width), 1)
    for start in range(0, cols, width):
        hit = columns + start == target_ref[...]
        part = lax.dot_general(
            weight_ref[:, start : start + width],
            jnp.where(hit, 1.0, 0.0).astype(jnp.bfloat16),
            (((1,), (1,)), ((), ())),
            preferred_element_type=jnp.float32,
        )
        if start == 0:
            sum_ref[...] = part
        else:
            sum_ref[...] += part
    bit = spot_ref[0] % 2
    for group in range(keep_ref.shape[0] // feats):
        out = pl.ds(group * feats, feats)
        near = pl.multiple_of((2 * group + bit) * feats, 8)
        far = pl.multiple_of((2 * group + 1 - bit) * feats, 8)
        keep_ref[out, :] = sum_ref[pl.ds(near, feats), :].astype(jnp.bfloat16)
        send_ref[out, :] = sum_ref[pl.ds(far, feats), :].astype(jnp.bfloat16)


def pick_next_kernel(feats, spot_ref, old_ref, got_ref, keep_ref, send_ref):
    def value(group):
        rows = pl.ds(pl.multiple_of(group * feats, 16), feats)
        return old_ref[rows, :] + got_ref[rows, :]

    bit = (spot_ref[0] // 2) % 2
    for group in range(keep_ref.shape[0] // feats):
        out = pl.ds(group * feats, feats)
        keep_ref[out, :] = value(2 * group + bit)
        send_ref[out, :] = value(2 * group + 1 - bit)


def pick_spread_kernel(feats, spot_ref, old_ref, got_ref, *outs):
    place = spot_ref[0] // 4
    rows = outs[0].shape[1]
    for shift in range(4):
        chosen = place ^ shift
        group = pl.ds(pl.multiple_of((chosen % 2) * feats, 16), feats)
        value = old_ref[group, :].astype(jnp.float32) + got_ref[group, :].astype(jnp.float32)
        value = jnp.where(chosen // 2 == 0, value[:, :rows], value[:, rows:])
        outs[shift][...] = value.astype(jnp.bfloat16)


def pick(where, local_targets, head_weight, count):
    tokens = local_targets.shape[0]
    depth, cols = head_weight.shape
    feats = 2 * depth // count
    rows = tokens // 2
    bf16 = jnp.bfloat16
    keep, send = pl.pallas_call(
        functools.partial(pick_kernel, feats),
        out_shape=[jax.ShapeDtypeStruct((depth // 2, tokens), bf16)] * 2,
        in_specs=[pl.BlockSpec(memory_space=pltpu.SMEM)] + vmem_specs(2),
        out_specs=vmem_specs(2),
        scratch_shapes=[pltpu.VMEM((depth, tokens), jnp.float32)],
        compiler_params=pltpu.CompilerParams(vmem_limit_bytes=14 * mebi),
        cost_estimate=pl.CostEstimate(
            flops=2 * depth * tokens * cols,
            transcendentals=0,
            bytes_accessed=2 * depth * cols,
        ),
    )(where, local_targets, head_weight)
    got = across(send, count, 1)
    keep, send = small_call(
        functools.partial(pick_next_kernel, feats),
        [((depth // 4, tokens), bf16)] * 2,
        [where, keep, got],
    )
    got = across(send, count, 2)
    keep, *sends = small_call(
        functools.partial(pick_spread_kernel, feats),
        [((feats, rows), bf16)] * 4,
        [where, keep, got],
    )
    return [keep] + [across(send, count, 4 * shift) for shift, send in zip((1, 2, 3), sends)]


def side_kernel(cols, place_ref, own_ref, other_ref, rows_ref, target_ref):
    swap = place_ref[1] != 0
    own, other = own_ref[...], other_ref[...]
    both = jnp.concatenate(
        [jnp.where(swap, other, own), jnp.where(swap, own, other)], axis=1
    )
    rows_ref[...] = both
    target_ref[...] = both.T[:, 0:1].astype(jnp.int32) - place_ref[0] * cols


def vmem_specs(number):
    return [pl.BlockSpec(memory_space=pltpu.VMEM)] * number


def split_rows(rows):
    high = rows.astype(jnp.bfloat16)
    rest = rows - high.astype(jnp.float32)
    middle = rest.astype(jnp.bfloat16)
    low = (rest - middle.astype(jnp.float32)).astype(jnp.bfloat16)
    return [high, middle, low]


def put_stats(ref, start, rows):
    for index, block in enumerate(split_rows(jnp.concatenate([rows, rows], axis=0))):
        ref[start + 16 * index : start + 16 * index + 16, :] = block


def get_stats(ref, start):
    blocks = [
        ref[start + 16 * index : start + 16 * index + 16, :].astype(jnp.float32)[0:8]
        for index in range(3)
    ]
    return blocks[0] + blocks[1] + blocks[2]


def merged_rows(bit, own, other):
    swap = bit != 0
    first = jnp.where(swap, other, own)
    second = jnp.where(swap, own, other)
    top = jnp.maximum(first[0:1], second[0:1])
    total = first[1:2] * jnp.exp(first[0:1] - top) + second[1:2] * jnp.exp(second[0:1] - top)
    target = first[2:3] + second[2:3]
    return jnp.concatenate([top, total, target, jnp.zeros((5, own.shape[1]), own.dtype)], axis=0)


def first_half_kernel(feats, spot_ref, grad_ref, stats_ref, keep_ref, send_ref):
    bit = spot_ref[0] % 2
    groups = keep_ref.shape[0] // feats
    for group in range(groups):
        out = pl.ds(group * feats, feats)
        near = pl.multiple_of((2 * group + bit) * feats, 8)
        far = pl.multiple_of((2 * group + 1 - bit) * feats, 8)
        keep_ref[out, :] = grad_ref[pl.ds(near, feats), :]
        send_ref[out, :] = grad_ref[pl.ds(far, feats), :].astype(jnp.bfloat16)
    put_stats(send_ref, groups * feats, stats_ref[...])


def halved(old_ref, got_ref, stats_ref, bit):
    own = stats_ref[...]
    other = get_stats(got_ref, old_ref.shape[0])
    merged = merged_rows(bit, own, other)
    return merged, jnp.exp(own[0:1] - merged[0:1]), jnp.exp(other[0:1] - merged[0:1])


def next_half_kernel(
    feats, mask, spot_ref, old_ref, got_ref, stats_ref, keep_ref, send_ref, new_stats_ref
):
    spot = spot_ref[0]
    merged, own_factor, other_factor = halved(old_ref, got_ref, stats_ref, (spot // mask) % 2)

    def value(group):
        rows = pl.ds(pl.multiple_of(group * feats, 16), feats)
        return old_ref[rows, :] * own_factor + got_ref[rows, :].astype(jnp.float32) * other_factor

    bit = (spot // (2 * mask)) % 2
    groups = keep_ref.shape[0] // feats
    for group in range(groups):
        out = pl.ds(group * feats, feats)
        keep_ref[out, :] = value(2 * group + bit)
        send_ref[out, :] = value(2 * group + 1 - bit).astype(jnp.bfloat16)
    put_stats(send_ref, groups * feats, merged)
    new_stats_ref[...] = merged


def spread_kernel(feats, spot_ref, old_ref, got_ref, stats_ref, keep_ref, new_stats_ref, *sends):
    spot = spot_ref[0]
    merged, own_factor, other_factor = halved(old_ref, got_ref, stats_ref, (spot // 2) % 2)
    new_stats_ref[...] = merged
    place = spot // 4
    rows = keep_ref.shape[1]
    for shift in range(4):
        chosen = place ^ shift
        group = pl.ds(pl.multiple_of((chosen % 2) * feats, 16), feats)
        left = chosen // 2 == 0
        value = old_ref[group, :] * own_factor + got_ref[group, :].astype(jnp.float32) * other_factor
        value = jnp.where(left, value[:, :rows], value[:, rows:])
        if shift == 0:
            keep_ref[...] = value
        else:
            send_ref = sends[shift - 1]
            send_ref[0:feats, :] = value.astype(jnp.bfloat16)
            put_stats(send_ref, feats, merged[:, :rows])
            put_stats(send_ref, feats + 48, merged[:, rows:])


def finish_kernel(
    span,
    pair_total,
    spot_ref,
    keep_ref,
    one_ref,
    two_ref,
    three_ref,
    stats_ref,
    picked_a_ref,
    picked_b_ref,
    picked_c_ref,
    picked_d_ref,
    rows_ref,
    grad_ref,
    columns_ref,
    margins_ref,
):
    feats, rows = keep_ref.shape
    place = spot_ref[0] // 4
    sent = [one_ref, two_ref, three_ref]
    quads = [stats_ref[...]] + [
        jnp.concatenate([get_stats(ref, feats), get_stats(ref, feats + 48)], axis=1) for ref in sent
    ]
    low = place % 2
    pair_one = merged_rows(low, quads[0], quads[1])
    pair_two = merged_rows(low, quads[2], quads[3])
    final = merged_rows(place // 2, pair_one, pair_two)
    top, total, target = final[0:1], final[1:2], final[2:3]
    weights = rows_ref[1:2, :]
    pair_local = pair_total // 2
    scored = (target - (top + jnp.log(total))) * weights
    sequence = lax.broadcasted_iota(jnp.int32, scored.shape, 1) // span
    lane = lax.broadcasted_iota(jnp.int32, (8, 128), 1)
    coef = jnp.zeros_like(scored)
    margins_out = losses_out = jnp.zeros(lane.shape, jnp.float32)

    def lane_of(pair):
        place = (pair // pair_local) * rows + pair % pair_local
        return slice(place, place + 1)

    for pair in range(pair_total):
        sums = [
            jnp.sum(jnp.where(sequence == 2 * pair + side, scored, 0.0), axis=1, keepdims=True)
            - rows_ref[3 + side : 4 + side, lane_of(pair)]
            for side in range(2)
        ]
        margin = beta_scale * (sums[0] - sums[1])
        winner = rows_ref[2:3, lane_of(pair)]
        loss, slope = pair_terms(margin, winner)
        scaled = beta_scale * grad_scale / pair_total * slope
        coef = jnp.where(sequence == 2 * pair, scaled, coef)
        coef = jnp.where(sequence == 2 * pair + 1, -scaled, coef)
        margins_out = jnp.where(lane == pair, margin, margins_out)
        losses_out = jnp.where(lane == pair, loss, losses_out)
    coef = coef * weights
    margins_ref[0:8, :] = margins_out
    margins_ref[8:16, :] = losses_out
    inverse = 1.0 / total
    blank = jnp.zeros((5, coef.shape[1]), jnp.float32)
    columns_ref[...] = jnp.concatenate([coef, top, inverse, blank], axis=0).T

    left = place // 2 == 0

    def own_block(row):
        return jnp.where(left, row[:, :rows], row[:, rows:])

    value = keep_ref[...] * own_block(jnp.exp(quads[0][0:1] - top))
    for ref, quad in zip(sent, quads[1:]):
        value = value + ref[0:feats, :].astype(jnp.float32) * own_block(jnp.exp(quad[0:1] - top))
    picked = sum(
        ref[...].astype(jnp.float32)
        for ref in (picked_a_ref, picked_b_ref, picked_c_ref, picked_d_ref)
    )
    picked_coef = coef * (1.0 - jnp.exp(target - top) * inverse)
    grad_ref[...] = (
        own_block(picked_coef) * picked
        - own_block(coef * inverse) * value
    ).astype(jnp.bfloat16)


def small_call(kernel, outs, args):
    return pl.pallas_call(
        kernel,
        out_shape=[jax.ShapeDtypeStruct(shape, dtype) for shape, dtype in outs],
        in_specs=[pl.BlockSpec(memory_space=pltpu.SMEM)] + vmem_specs(len(args) - 1),
        out_specs=vmem_specs(len(outs)),
        compiler_params=pltpu.CompilerParams(vmem_limit_bytes=12 * mebi),
        cost_estimate=pl.CostEstimate(flops=0, transcendentals=0, bytes_accessed=2000000),
    )(*args)


def finish(grad, stats, picked, rows_info, where, count, span, pair_total):
    depth, tokens = grad.shape
    feats = 2 * depth // count
    rows = tokens // 2
    f32, bf16 = jnp.float32, jnp.bfloat16
    half, quarter = depth // 2, depth // 4
    keep, send = small_call(
        functools.partial(first_half_kernel, feats),
        [((half, tokens), f32), ((half + 48, tokens), bf16)],
        [where, grad, stats],
    )
    got = across(send, count, 1)
    keep, send, stats = small_call(
        functools.partial(next_half_kernel, feats, 1),
        [((quarter, tokens), f32), ((quarter + 48, tokens), bf16), ((8, tokens), f32)],
        [where, keep, got, stats],
    )
    got = across(send, count, 2)
    keep, stats, *sends = small_call(
        functools.partial(spread_kernel, feats),
        [((feats, rows), f32), ((8, tokens), f32)] + [((feats + 96, rows), bf16)] * 3,
        [where, keep, got, stats],
    )
    gots = [across(send, count, 4 * shift) for shift, send in zip((1, 2, 3), sends)]
    return small_call(
        functools.partial(finish_kernel, span, pair_total),
        [((feats, rows), bf16), ((tokens, 8), f32), ((16, 128), f32)],
        [where, keep, *gots, stats, *picked, rows_info],
    )


def head_kernel(first, hidden_ref, logits_ref, rows_ref, target_ref, *rest):
    out_ref = rest[-1]
    width = out_ref.shape[1]
    coef, top, inverse = rows_ref[:, 0:1], rows_ref[:, 1:2], rows_ref[:, 2:3]
    start = (pl.program_id(0) + first) * width
    columns = lax.broadcasted_iota(jnp.int32, logits_ref.shape, 1) + start
    onehot = jnp.where(columns == target_ref[...], 1.0, 0.0)
    probs = jnp.exp(logits_ref[...] - top) * inverse
    dlogits = (coef * (onehot - probs)).astype(jnp.bfloat16)
    depth = out_ref.shape[0]
    step = 256 if depth % 256 == 0 else depth
    for start in range(0, depth, step):
        out_ref[start : start + step, :] = jnp.dot(
            hidden_ref[start : start + step, :], dlogits, preferred_element_type=jnp.float32
        ).astype(out_ref.dtype)


def head_blocks(hidden_t, logits, row_values, local_targets):
    depth, tokens = hidden_t.shape
    cols = logits.shape[1]
    width = cols // 4 if cols % 512 == 0 else cols
    steps = cols // width
    groups = (steps,)
    out = None
    first = 0
    for count in groups:
        whole = lambda step: (0, 0)
        column = lambda step, first=first: (0, step + first)
        in_specs = [
            pl.BlockSpec((depth, tokens), whole),
            pl.BlockSpec((tokens, width), column),
            pl.BlockSpec((tokens, 8), whole),
            pl.BlockSpec((tokens, 1), whole),
        ]
        args = [hidden_t, logits, row_values, local_targets]
        aliases = {}
        if out is not None:
            in_specs.append(pl.BlockSpec(memory_space=pl.ANY))
            args.append(out)
            aliases = {4: 0}
        out = pl.pallas_call(
            lambda *refs, first=first: head_kernel(first, *refs),
            out_shape=jax.ShapeDtypeStruct((depth, cols), jnp.bfloat16),
            grid=(count,),
            in_specs=in_specs,
            out_specs=pl.BlockSpec((depth, width), column),
            input_output_aliases=aliases,
            compiler_params=pltpu.CompilerParams(vmem_limit_bytes=16 * mebi),
            cost_estimate=pl.CostEstimate(
                flops=2 * depth * tokens * width * count,
                transcendentals=tokens * width * count,
                bytes_accessed=(2 * depth + 4 * tokens) * width * count,
            ),
        )(*args)
        first += count
    return out


def part_widths(cols):
    unit = cols // (128 * sum(part_tiles)) * 128
    if unit == 0 or unit * sum(part_tiles) != cols:
        return (cols,)
    return tuple(unit * tile for tile in part_tiles)


def paired_local(hidden, head_weight, targets, response_mask, labels, reference_sums):
    return paired_body(
        hidden, head_weight, targets, response_mask, labels, reference_sums
    )


def paired_body(hidden, head_weight, targets, response_mask, labels, reference_sums):
    rows = hidden.shape[0]
    depth, cols = head_weight.shape
    pair_local = labels.shape[0]
    pair_total = 2 * pair_local
    span = rows // (2 * pair_local)
    count = lax.axis_size("vocab")
    half = count // 2
    plane = lax.axis_index("tok")
    spot = lax.axis_index("vocab")
    moves = spot // half != plane

    where = jnp.stack([spot, plane]).astype(jnp.int32)
    info = jnp.concatenate(
        [
            targets.astype(jnp.float32)[None],
            response_mask.astype(jnp.float32)[None],
            jnp.pad(labels.astype(jnp.float32)[None], ((0, 0), (0, rows - pair_local))),
            jnp.pad(reference_sums.T, ((0, 0), (0, rows - pair_local))),
            jnp.zeros((3, rows), jnp.float32),
        ],
        axis=0,
    )
    where, moves, info, head_weight = lax.optimization_barrier((where, moves, info, head_weight))
    piece = plane_swap(hidden.T, count, moves)
    head_weight = load(head_weight)
    hidden_t, hidden_n = gather_hidden(piece, where, count)
    rows_info, local_targets = small_call(
        functools.partial(side_kernel, cols),
        [((8, 2 * rows), jnp.float32), ((2 * rows, 1), jnp.int32)],
        [where, info, over(info)],
    )
    picked = pick(where, local_targets, head_weight, count)

    scale = 1.0
    while hidden_bound * weight_bound * depth * scale > half_limit:
        scale *= 0.5
    widths = part_widths(cols)
    starts = [sum(widths[:part]) for part in range(len(widths))]
    swapped = []
    for start, width in zip(starts, widths):
        own = logit_part(start, width, hidden_n, head_weight)
        sent = (own * scale if scale != 1.0 else own).astype(jnp.float16)
        got = over(sent)
        swapped.append((own, got))
    logit_parts = []
    state = None
    for part, (start, width) in enumerate(zip(starts, widths)):
        own, got = swapped[part]
        got = got.astype(jnp.float32)
        logits = own + (got * (1.0 / scale) if scale != 1.0 else got)
        logit_parts.append(logits)
        state = fold(start, width, logits, local_targets, head_weight, state)
        if part == len(widths) - 2:
            state, picked = lax.optimization_barrier((state, picked))
    stats, grad = state
    hidden_part, row_values, margin_rows = finish(
        grad, stats, picked, rows_info, where, count, span, pair_total
    )
    hidden_grad = plane_swap(hidden_part, count, moves).T
    other_rows = over(margin_rows)
    logits = jnp.concatenate(logit_parts, axis=1)
    head_grad = head_blocks(hidden_t, logits, row_values, local_targets)
    margins_all = margin_rows[0, :pair_total]
    margins = jnp.where(plane == 0, margins_all[:pair_local], margins_all[pair_local:])
    own_losses, other_losses = margin_rows[8], other_rows[8]
    lane_plane = lax.broadcasted_iota(jnp.int32, (128,), 0) // pair_local
    losses = jnp.where(lane_plane == plane, own_losses, other_losses)
    mean_loss = jnp.sum(losses[:pair_total]) / pair_total
    return (mean_loss, margins, hidden_grad, head_grad)


def solution(mesh):
    count = mesh.shape["vocab"]
    paired = mesh.shape["tok"] == 2 and count == 16
    return jax.shard_map(
        paired_local if paired else general_local,
        mesh=mesh,
        in_specs=(
            P("tok", "vocab"),
            P("tok", "vocab"),
            P("tok"),
            P("tok"),
            P("tok"),
            P("tok", None),
        ),
        out_specs=(P(), P("tok"), P("tok", "vocab"), P("tok", "vocab")),
        check_vma=False,
    )
```

```python
import functools
import math

import jax
import jax.numpy as jnp
from jax import lax
from jax.experimental import pallas as pl
from jax.experimental.pallas import tpu as pltpu
from jax.sharding import PartitionSpec as P


beta_scale = 0.1
tie_offset = math.log(2.0)
tie_const = math.log(3.0)
grad_scale = 512.0


def pair_terms(margins, labels):
    winner = labels.astype(jnp.float32)
    log_tie = (
        tie_const
        + margins
        - tie_offset
        - jax.nn.softplus(margins - tie_offset)
        - jax.nn.softplus(margins + tie_offset)
    )
    losses = winner * jax.nn.softplus(tie_offset - margins) - (1.0 - winner) * log_tie
    slopes = -winner * jax.nn.sigmoid(tie_offset - margins) - (1.0 - winner) * (
        1.0 - jax.nn.sigmoid(margins - tie_offset) - jax.nn.sigmoid(margins + tie_offset)
    )
    return (losses, slopes)


def add_parts(received):
    return jnp.sum(received, axis=0)


def general_local(hidden, head_weight, targets, response_mask, labels, reference_sums):
    tok_rows = hidden.shape[0]
    vocab_cols = head_weight.shape[1]
    tok_count = lax.axis_size("tok")
    pair_local = labels.shape[0]
    pair_total = pair_local * tok_count
    span = tok_rows // (2 * pair_local)
    rows_full = lax.all_gather(hidden, "vocab", axis=1, tiled=True)
    token_cols = lax.all_to_all(rows_full, "tok", split_axis=1, concat_axis=0, tiled=True)
    partial_value = jnp.dot(token_cols, head_weight, preferred_element_type=jnp.float32)
    partial_value = partial_value.reshape(tok_count, tok_rows, vocab_cols)
    logits = add_parts(
        lax.all_to_all(partial_value, "tok", split_axis=0, concat_axis=0, tiled=True)
    )
    offset = lax.axis_index("vocab") * vocab_cols
    columns = lax.broadcasted_iota(jnp.int32, (1, vocab_cols), 1) + offset
    matched = columns == targets[:, None]
    local_max = jnp.max(logits, axis=1)
    local_target = jnp.sum(jnp.where(matched, logits, 0.0), axis=1)
    row_max = lax.pmax(local_max, "vocab")
    shifted = jnp.exp(logits - row_max[:, None])
    totals, target_logit = lax.psum((jnp.sum(shifted, axis=1), local_target), "vocab")
    probs = shifted / totals[:, None]
    token_logp = target_logit - (row_max + jnp.log(totals))
    weights = response_mask.astype(jnp.float32)
    sequence_logp = jnp.sum((token_logp * weights).reshape(pair_local, 2, span), axis=2)
    ratios = sequence_logp - reference_sums
    margins = beta_scale * (ratios[:, 0] - ratios[:, 1])
    losses, slopes = pair_terms(margins, labels)
    mean_loss = lax.psum(jnp.sum(losses), "tok") / pair_total
    pair_coef = beta_scale * grad_scale / pair_total * slopes
    signed = jnp.stack([pair_coef, -pair_coef], axis=1)
    token_coef = (
        jnp.broadcast_to(signed[:, :, None], (pair_local, 2, span)).reshape(tok_rows) * weights
    )
    onehot = jnp.where(matched, 1.0, 0.0).astype(jnp.float32)
    dlogits = (token_coef[:, None] * (onehot - probs)).astype(jnp.bfloat16)
    dlogit_all = lax.all_gather(dlogits, "tok", axis=0, tiled=True)
    head_grad = lax.dot_general(
        token_cols, dlogit_all, (((0,), (0,)), ((), ())), preferred_element_type=jnp.float32
    ).astype(jnp.bfloat16)
    partial_grad = lax.dot_general(
        head_weight, dlogit_all, (((1,), (1,)), ((), ())), preferred_element_type=jnp.float32
    )
    returned = lax.all_to_all(
        partial_grad.astype(jnp.bfloat16), "tok", split_axis=1, concat_axis=0, tiled=True
    ).astype(partial_grad.dtype)
    grad_cols = lax.psum_scatter(returned, "vocab", scatter_dimension=0, tiled=True)
    hidden_grad = grad_cols.T.astype(jnp.bfloat16)
    return (mean_loss, margins, hidden_grad, head_grad)


swap_pairs = ((0, 1), (1, 0))
hidden_bound = 8.0
weight_bound = 4.0
half_limit = 60000.0
part_tiles = (4, 4, 8, 8, 8, 4, 4)
mebi = 1 << 20
stats_rows = 16


def exclusive(count, mask):
    return [(spot, spot ^ mask) for spot in range(count)]


def across(value, count, mask):
    return lax.ppermute(value, "vocab", exclusive(count, mask))


def over(value):
    return lax.ppermute(value, "tok", swap_pairs)


def plane_swap(value, count, moves):
    half = count // 2
    pairs = []
    for plane in range(2):
        for spot in range(count):
            if spot // half != plane:
                pairs.append((2 * spot + plane, 2 * (spot ^ half) + 1 - plane))
    received = lax.ppermute(value, ("vocab", "tok"), pairs)
    return received if moves is None else jnp.where(moves, received, value)


def place_kernel(order, spot_ref, *refs):
    hidden_t_ref, hidden_n_ref = refs[-2:]
    slots, feats, rows = refs[0].shape
    half = 2 * slots
    spot = spot_ref[0]
    for side, ref in zip((0, 2, 1, 3), refs[:-2]):
        for slot in range(slots):
            source = spot ^ (order[slot] ^ side)
            start = pl.multiple_of((source % half) * feats, 32)
            column = pl.multiple_of((source // half) * rows, 128)
            hidden_t_ref[pl.ds(start, feats), pl.ds(column, rows)] = ref[slot]
    depth = hidden_t_ref.shape[0]
    step = 256 if depth % 256 == 0 else 128
    for start in range(0, depth, step):
        hidden_n_ref[:, start : start + step] = hidden_t_ref[start : start + step, :].T


def fold_kernel(start, has_state, logits_ref, target_ref, weight_ref, *refs):
    if has_state:
        stats_ref, grad_ref, new_stats_ref, new_grad_ref, terms_ref = refs
    else:
        new_stats_ref, new_grad_ref, terms_ref = refs
    logits = logits_ref[...]
    width = logits.shape[1]
    columns = lax.broadcasted_iota(jnp.int32, logits.shape, 1) + start
    hit = columns == target_ref[...]
    top = jnp.max(logits, axis=1, keepdims=True)
    if has_state:
        old = stats_ref[...].T
        old_top = old[:, 0:1]
        top = jnp.maximum(top, old_top)
    terms = jnp.exp(logits - top)
    total = jnp.sum(terms, axis=1, keepdims=True)
    target = jnp.sum(jnp.where(hit, logits, 0.0), axis=1, keepdims=True)
    terms_ref[...] = jnp.where(hit, 0.0, terms).astype(jnp.bfloat16)
    shrink = jnp.ones_like(top)
    if has_state:
        shrink = jnp.exp(old_top - top)
        total = total + old[:, 1:2] * shrink
        target = target + old[:, 2:3]
    lane = lax.broadcasted_iota(jnp.int32, (logits.shape[0], 128), 1)
    packed = jnp.where(
        lane == 0, top, jnp.where(lane == 1, total, jnp.where(lane == 2, target, shrink))
    ).T
    new_stats_ref[...] = packed[0:8]
    shrink_row = packed[3:4]
    depth = weight_ref.shape[0]
    step = depth // 2 if depth % 256 == 0 else depth
    for first in range(0, depth, step):
        part = lax.dot_general(
            weight_ref[first : first + step, start : start + width],
            terms_ref[...],
            (((1,), (1,)), ((), ())),
            preferred_element_type=jnp.float32,
        )
        if has_state:
            part = part + grad_ref[first : first + step, :] * shrink_row
        new_grad_ref[first : first + step, :] = part


def fold(start, width, logits, local_targets, head_weight, state):
    tokens = logits.shape[0]
    depth = head_weight.shape[0]
    args = [logits, local_targets, head_weight]
    aliases = {}
    if state is not None:
        args += list(state)
        aliases = {4: 1}
    return pl.pallas_call(
        functools.partial(fold_kernel, start, state is not None),
        out_shape=(
            jax.ShapeDtypeStruct((8, tokens), jnp.float32),
            jax.ShapeDtypeStruct((depth, tokens), jnp.float32),
        ),
        in_specs=vmem_specs(len(args)),
        out_specs=tuple(vmem_specs(2)),
        scratch_shapes=[pltpu.VMEM((tokens, width), jnp.bfloat16)],
        input_output_aliases=aliases,
        compiler_params=pltpu.CompilerParams(vmem_limit_bytes=12 * mebi),
        cost_estimate=pl.CostEstimate(
            flops=2 * depth * tokens * width,
            transcendentals=tokens * width,
            bytes_accessed=2 * depth * width + 4 * tokens * width + 8 * depth * tokens,
        ),
    )(*args)


def load_kernel(source_ref, held_ref, sems):
    number = sems.shape[0]
    rows = source_ref.shape[0] // number
    copies = [
        pltpu.make_async_copy(
            source_ref.at[pl.ds(index * rows, rows)],
            held_ref.at[pl.ds(index * rows, rows)],
            sems.at[index],
        )
        for index in range(number)
    ]
    for copy in copies:
        copy.start()
    for copy in copies:
        copy.wait()


def load(head_weight):
    depth = head_weight.shape[0]
    number = 8 if depth % 256 == 0 else 1
    return pl.pallas_call(
        load_kernel,
        out_shape=pltpu.VMEM(head_weight.shape, head_weight.dtype),
        in_specs=[pl.BlockSpec(memory_space=pl.ANY)],
        out_specs=pl.BlockSpec(memory_space=pltpu.VMEM),
        scratch_shapes=[pltpu.SemaphoreType.DMA((number,))],
        compiler_params=pltpu.CompilerParams(vmem_limit_bytes=20 * mebi),
        cost_estimate=pl.CostEstimate(
            flops=0, transcendentals=0, bytes_accessed=2 * head_weight.size
        ),
    )(head_weight)


def logit_kernel(start, hidden_ref, weight_ref, out_ref):
    width = out_ref.shape[1]
    step = 256 if width % 256 == 0 else width
    for first in range(0, width, step):
        out_ref[:, first : first + step] = jnp.dot(
            hidden_ref[...],
            weight_ref[:, start + first : start + first + step],
            preferred_element_type=jnp.float32,
        )


def logit_part(start, width, hidden_n, head_weight):
    tokens, depth = hidden_n.shape
    return pl.pallas_call(
        functools.partial(logit_kernel, start),
        out_shape=jax.ShapeDtypeStruct((tokens, width), jnp.float32),
        in_specs=vmem_specs(2),
        out_specs=vmem_specs(1)[0],
        compiler_params=pltpu.CompilerParams(vmem_limit_bytes=12 * mebi),
        cost_estimate=pl.CostEstimate(
            flops=2 * depth * tokens * width, transcendentals=0, bytes_accessed=2 * depth * width
        ),
    )(hidden_n, head_weight)


def gather_hidden(piece, where, count):
    order = [0]
    parts = [piece]
    for mask in range(4, count, 4):
        order.append(mask)
        parts.append(across(piece, count, mask))
    feats, rows = piece.shape
    stacked = jnp.concatenate(parts, axis=0)
    side = across(stacked, count, 2)
    groups = [stacked, side, across(stacked, count, 1), across(side, count, 1)]
    slots = len(order)
    depth = 2 * slots * feats
    return pl.pallas_call(
        lambda *refs: place_kernel(order, *refs),
        out_shape=(
            jax.ShapeDtypeStruct((depth, 2 * rows), piece.dtype),
            jax.ShapeDtypeStruct((2 * rows, depth), piece.dtype),
        ),
        in_specs=[pl.BlockSpec(memory_space=pltpu.SMEM)]
        + [pl.BlockSpec(memory_space=pltpu.VMEM)] * len(groups),
        out_specs=[pl.BlockSpec(memory_space=pltpu.VMEM)] * 2,
        compiler_params=pltpu.CompilerParams(vmem_limit_bytes=8 * mebi),
        cost_estimate=pl.CostEstimate(flops=0, transcendentals=0, bytes_accessed=4000000),
    )(
        where,
        *[group.reshape(slots, feats, rows) for group in groups],
    )


def pick_kernel(feats, spot_ref, target_ref, weight_ref, keep_ref, send_ref, sum_ref):
    _, cols = weight_ref.shape
    width = 1024 if cols % 1024 == 0 else cols
    columns = lax.broadcasted_iota(jnp.int32, (target_ref.shape[0], width), 1)
    for start in range(0, cols, width):
        hit = columns + start == target_ref[...]
        part = lax.dot_general(
            weight_ref[:, start : start + width],
            jnp.where(hit, 1.0, 0.0).astype(jnp.bfloat16),
            (((1,), (1,)), ((), ())),
            preferred_element_type=jnp.float32,
        )
        if start == 0:
            sum_ref[...] = part
        else:
            sum_ref[...] += part
    bit = spot_ref[0] % 2
    for group in range(keep_ref.shape[0] // feats):
        out = pl.ds(group * feats, feats)
        near = pl.multiple_of((2 * group + bit) * feats, 8)
        far = pl.multiple_of((2 * group + 1 - bit) * feats, 8)
        keep_ref[out, :] = sum_ref[pl.ds(near, feats), :].astype(jnp.bfloat16)
        send_ref[out, :] = sum_ref[pl.ds(far, feats), :].astype(jnp.bfloat16)


def pick_next_kernel(feats, spot_ref, old_ref, got_ref, keep_ref, send_ref):
    def value(group):
        rows = pl.ds(pl.multiple_of(group * feats, 16), feats)
        return old_ref[rows, :] + got_ref[rows, :]

    bit = (spot_ref[0] // 2) % 2
    for group in range(keep_ref.shape[0] // feats):
        out = pl.ds(group * feats, feats)
        keep_ref[out, :] = value(2 * group + bit)
        send_ref[out, :] = value(2 * group + 1 - bit)


def pick_spread_kernel(feats, spot_ref, old_ref, got_ref, *outs):
    place = spot_ref[0] // 4
    rows = outs[0].shape[1]
    for shift in range(4):
        chosen = place ^ shift
        group = pl.ds(pl.multiple_of((chosen % 2) * feats, 16), feats)
        value = old_ref[group, :].astype(jnp.float32) + got_ref[group, :].astype(jnp.float32)
        value = jnp.where(chosen // 2 == 0, value[:, :rows], value[:, rows:])
        outs[shift][...] = value.astype(jnp.bfloat16)


def pick(where, local_targets, head_weight, count):
    tokens = local_targets.shape[0]
    depth, cols = head_weight.shape
    feats = 2 * depth // count
    rows = tokens // 2
    bf16 = jnp.bfloat16
    keep, send = pl.pallas_call(
        functools.partial(pick_kernel, feats),
        out_shape=[jax.ShapeDtypeStruct((depth // 2, tokens), bf16)] * 2,
        in_specs=[pl.BlockSpec(memory_space=pltpu.SMEM)] + vmem_specs(2),
        out_specs=vmem_specs(2),
        scratch_shapes=[pltpu.VMEM((depth, tokens), jnp.float32)],
        compiler_params=pltpu.CompilerParams(vmem_limit_bytes=14 * mebi),
        cost_estimate=pl.CostEstimate(
            flops=2 * depth * tokens * cols,
            transcendentals=0,
            bytes_accessed=2 * depth * cols,
        ),
    )(where, local_targets, head_weight)
    got = across(send, count, 1)
    keep, send = small_call(
        functools.partial(pick_next_kernel, feats),
        [((depth // 4, tokens), bf16)] * 2,
        [where, keep, got],
    )
    got = across(send, count, 2)
    keep, *sends = small_call(
        functools.partial(pick_spread_kernel, feats),
        [((feats, rows), bf16)] * 4,
        [where, keep, got],
    )
    return [keep] + [across(send, count, 4 * shift) for shift, send in zip((1, 2, 3), sends)]


def side_kernel(cols, place_ref, own_ref, other_ref, rows_ref, target_ref):
    swap = place_ref[1] != 0
    own, other = own_ref[...], other_ref[...]
    both = jnp.concatenate(
        [jnp.where(swap, other, own), jnp.where(swap, own, other)], axis=1
    )
    rows_ref[...] = both
    target_ref[...] = both.T[:, 0:1].astype(jnp.int32) - place_ref[0] * cols


def vmem_specs(number):
    return [pl.BlockSpec(memory_space=pltpu.VMEM)] * number


def put_stats(ref, start, rows):
    rows = rows[0:3]
    high = rows.astype(jnp.bfloat16).astype(jnp.float32)
    rest = rows - high
    middle = rest.astype(jnp.bfloat16).astype(jnp.float32)
    blank = jnp.zeros((stats_rows - 9, rows.shape[1]), jnp.float32)
    block = jnp.concatenate([high, middle, rest - middle, blank], axis=0)
    ref[start : start + stats_rows, :] = block.astype(jnp.bfloat16)


def get_stats(ref, start):
    block = ref[start : start + stats_rows, :].astype(jnp.float32)
    blank = jnp.zeros((5, block.shape[1]), jnp.float32)
    return jnp.concatenate([block[0:3] + block[3:6] + block[6:9], blank], axis=0)


def merged_rows(bit, own, other):
    swap = bit != 0
    first = jnp.where(swap, other, own)
    second = jnp.where(swap, own, other)
    top = jnp.maximum(first[0:1], second[0:1])
    total = first[1:2] * jnp.exp(first[0:1] - top) + second[1:2] * jnp.exp(second[0:1] - top)
    target = first[2:3] + second[2:3]
    return jnp.concatenate([top, total, target, jnp.zeros((5, own.shape[1]), own.dtype)], axis=0)


def first_half_kernel(feats, spot_ref, grad_ref, stats_ref, keep_ref, send_ref):
    bit = spot_ref[0] % 2
    groups = keep_ref.shape[0] // feats
    for group in range(groups):
        out = pl.ds(group * feats, feats)
        near = pl.multiple_of((2 * group + bit) * feats, 8)
        far = pl.multiple_of((2 * group + 1 - bit) * feats, 8)
        keep_ref[out, :] = grad_ref[pl.ds(near, feats), :]
        send_ref[out, :] = grad_ref[pl.ds(far, feats), :].astype(jnp.bfloat16)
    put_stats(send_ref, groups * feats, stats_ref[...])


def halved(old_ref, got_ref, stats_ref, bit):
    own = stats_ref[...]
    other = get_stats(got_ref, old_ref.shape[0])
    merged = merged_rows(bit, own, other)
    return merged, jnp.exp(own[0:1] - merged[0:1]), jnp.exp(other[0:1] - merged[0:1])


def next_half_kernel(
    feats, mask, spot_ref, old_ref, got_ref, stats_ref, keep_ref, send_ref, new_stats_ref
):
    spot = spot_ref[0]
    merged, own_factor, other_factor = halved(old_ref, got_ref, stats_ref, (spot // mask) % 2)

    def value(group):
        rows = pl.ds(pl.multiple_of(group * feats, 16), feats)
        return old_ref[rows, :] * own_factor + got_ref[rows, :].astype(jnp.float32) * other_factor

    bit = (spot // (2 * mask)) % 2
    groups = keep_ref.shape[0] // feats
    for group in range(groups):
        out = pl.ds(group * feats, feats)
        keep_ref[out, :] = value(2 * group + bit)
        send_ref[out, :] = value(2 * group + 1 - bit).astype(jnp.bfloat16)
    put_stats(send_ref, groups * feats, merged)
    new_stats_ref[...] = merged


def spread_kernel(feats, spot_ref, old_ref, got_ref, stats_ref, keep_ref, new_stats_ref, *sends):
    spot = spot_ref[0]
    merged, own_factor, other_factor = halved(old_ref, got_ref, stats_ref, (spot // 2) % 2)
    new_stats_ref[...] = merged
    place = spot // 4
    rows = keep_ref.shape[1]
    for shift in range(4):
        chosen = place ^ shift
        group = pl.ds(pl.multiple_of((chosen % 2) * feats, 16), feats)
        left = chosen // 2 == 0
        value = old_ref[group, :] * own_factor + got_ref[group, :].astype(jnp.float32) * other_factor
        value = jnp.where(left, value[:, :rows], value[:, rows:])
        if shift == 0:
            keep_ref[...] = value
        else:
            send_ref = sends[shift - 1]
            send_ref[0:feats, :] = value.astype(jnp.bfloat16)
            put_stats(send_ref, feats, merged[:, :rows])
            put_stats(send_ref, feats + stats_rows, merged[:, rows:])


def finish_kernel(
    span,
    pair_total,
    spot_ref,
    keep_ref,
    one_ref,
    two_ref,
    three_ref,
    stats_ref,
    picked_a_ref,
    picked_b_ref,
    picked_c_ref,
    picked_d_ref,
    rows_ref,
    grad_ref,
    columns_ref,
    margins_ref,
):
    feats, rows = keep_ref.shape
    place = spot_ref[0] // 4
    sent = [one_ref, two_ref, three_ref]
    quads = [stats_ref[...]] + [
        jnp.concatenate([get_stats(ref, feats), get_stats(ref, feats + stats_rows)], axis=1) for ref in sent
    ]
    low = place % 2
    pair_one = merged_rows(low, quads[0], quads[1])
    pair_two = merged_rows(low, quads[2], quads[3])
    final = merged_rows(place // 2, pair_one, pair_two)
    top, total, target = final[0:1], final[1:2], final[2:3]
    weights = rows_ref[1:2, :]
    pair_local = pair_total // 2
    scored = (target - (top + jnp.log(total))) * weights
    sequence = lax.broadcasted_iota(jnp.int32, scored.shape, 1) // span
    lane = lax.broadcasted_iota(jnp.int32, (8, 128), 1)
    coef = jnp.zeros_like(scored)
    margins_out = losses_out = jnp.zeros(lane.shape, jnp.float32)

    def lane_of(pair):
        place = (pair // pair_local) * rows + pair % pair_local
        return slice(place, place + 1)

    for pair in range(pair_total):
        sums = [
            jnp.sum(jnp.where(sequence == 2 * pair + side, scored, 0.0), axis=1, keepdims=True)
            - rows_ref[3 + side : 4 + side, lane_of(pair)]
            for side in range(2)
        ]
        margin = beta_scale * (sums[0] - sums[1])
        winner = rows_ref[2:3, lane_of(pair)]
        loss, slope = pair_terms(margin, winner)
        scaled = beta_scale * grad_scale / pair_total * slope
        coef = jnp.where(sequence == 2 * pair, scaled, coef)
        coef = jnp.where(sequence == 2 * pair + 1, -scaled, coef)
        margins_out = jnp.where(lane == pair, margin, margins_out)
        losses_out = jnp.where(lane == pair, loss, losses_out)
    coef = coef * weights
    margins_ref[0:8, :] = margins_out
    margins_ref[8:16, :] = losses_out
    inverse = 1.0 / total
    blank = jnp.zeros((5, coef.shape[1]), jnp.float32)
    columns_ref[...] = jnp.concatenate([coef, top, inverse, blank], axis=0).T

    left = place // 2 == 0

    def own_block(row):
        return jnp.where(left, row[:, :rows], row[:, rows:])

    value = keep_ref[...] * own_block(jnp.exp(quads[0][0:1] - top))
    for ref, quad in zip(sent, quads[1:]):
        value = value + ref[0:feats, :].astype(jnp.float32) * own_block(jnp.exp(quad[0:1] - top))
    picked = sum(
        ref[...].astype(jnp.float32)
        for ref in (picked_a_ref, picked_b_ref, picked_c_ref, picked_d_ref)
    )
    picked_coef = coef * (1.0 - jnp.exp(target - top) * inverse)
    grad_ref[...] = (
        own_block(picked_coef) * picked
        - own_block(coef * inverse) * value
    ).astype(jnp.bfloat16)


def small_call(kernel, outs, args):
    return pl.pallas_call(
        kernel,
        out_shape=[jax.ShapeDtypeStruct(shape, dtype) for shape, dtype in outs],
        in_specs=[pl.BlockSpec(memory_space=pltpu.SMEM)] + vmem_specs(len(args) - 1),
        out_specs=vmem_specs(len(outs)),
        compiler_params=pltpu.CompilerParams(vmem_limit_bytes=12 * mebi),
        cost_estimate=pl.CostEstimate(flops=0, transcendentals=0, bytes_accessed=2000000),
    )(*args)


def finish(grad, stats, picked, rows_info, where, count, span, pair_total):
    depth, tokens = grad.shape
    feats = 2 * depth // count
    rows = tokens // 2
    f32, bf16 = jnp.float32, jnp.bfloat16
    half, quarter = depth // 2, depth // 4
    keep, send = small_call(
        functools.partial(first_half_kernel, feats),
        [((half, tokens), f32), ((half + stats_rows, tokens), bf16)],
        [where, grad, stats],
    )
    got = across(send, count, 1)
    keep, send, stats = small_call(
        functools.partial(next_half_kernel, feats, 1),
        [((quarter, tokens), f32), ((quarter + stats_rows, tokens), bf16), ((8, tokens), f32)],
        [where, keep, got, stats],
    )
    got = across(send, count, 2)
    keep, stats, *sends = small_call(
        functools.partial(spread_kernel, feats),
        [((feats, rows), f32), ((8, tokens), f32)] + [((feats + 2 * stats_rows, rows), bf16)] * 3,
        [where, keep, got, stats],
    )
    gots = [across(send, count, 4 * shift) for shift, send in zip((1, 2, 3), sends)]
    return small_call(
        functools.partial(finish_kernel, span, pair_total),
        [((feats, rows), bf16), ((tokens, 8), f32), ((16, 128), f32)],
        [where, keep, *gots, stats, *picked, rows_info],
    )


def head_kernel(hidden_ref, logits_ref, rows_ref, target_ref, out_ref):
    width = out_ref.shape[1]
    coef, top, inverse = rows_ref[:, 0:1], rows_ref[:, 1:2], rows_ref[:, 2:3]
    depth = out_ref.shape[0]
    rows = 256 if depth % 256 == 0 else depth
    part = 256 if width % 256 == 0 else width
    columns = lax.broadcasted_iota(jnp.int32, (logits_ref.shape[0], part), 1)
    start = pl.program_id(0) * width
    for column in range(0, width, part):
        onehot = jnp.where(columns + (start + column) == target_ref[...], 1.0, 0.0)
        probs = jnp.exp(logits_ref[:, column : column + part] - top) * inverse
        dlogits = (coef * (onehot - probs)).astype(jnp.bfloat16)
        for first in range(0, depth, rows):
            out_ref[first : first + rows, column : column + part] = jnp.dot(
                hidden_ref[first : first + rows, :],
                dlogits,
                preferred_element_type=jnp.float32,
            ).astype(out_ref.dtype)


def head_blocks(hidden_t, logits, row_values, local_targets):
    depth, tokens = hidden_t.shape
    cols = logits.shape[1]
    width = cols // 5 if cols % (5 * 256) == 0 else cols
    whole = lambda step: (0, 0)
    column = lambda step: (0, step)
    return pl.pallas_call(
        head_kernel,
        out_shape=jax.ShapeDtypeStruct((depth, cols), jnp.bfloat16),
        grid=(cols // width,),
        in_specs=[
            pl.BlockSpec((depth, tokens), whole),
            pl.BlockSpec((tokens, width), column),
            pl.BlockSpec((tokens, 8), whole),
            pl.BlockSpec((tokens, 1), whole),
        ],
        out_specs=pl.BlockSpec((depth, width), column),
        compiler_params=pltpu.CompilerParams(vmem_limit_bytes=40 * mebi),
        cost_estimate=pl.CostEstimate(
            flops=2 * depth * tokens * cols,
            transcendentals=tokens * cols,
            bytes_accessed=(2 * depth + 4 * tokens) * cols,
        ),
    )(hidden_t, logits, row_values, local_targets)


def last_kernel(pair_local, place_ref, rows_ref, other_ref, own_ref, got_ref, grad_ref, loss_ref, margin_ref):
    half = place_ref[2]
    plane = place_ref[1]
    first = plane == 0
    moved = jnp.where(
        place_ref[0] // half != plane,
        got_ref[...].astype(jnp.float32),
        own_ref[...].astype(jnp.float32),
    )
    grad_ref[...] = moved.astype(grad_ref.dtype)
    total = jnp.zeros((1, 1), jnp.float32)
    for pair in range(2 * pair_local):
        own, other = rows_ref[8:9, pair : pair + 1], other_ref[8:9, pair : pair + 1]
        total = total + jnp.where(first == (pair < pair_local), own, other)
    loss_ref[...] = total / (2 * pair_local)
    margin_ref[...] = jnp.where(
        first, rows_ref[0:1, 0:pair_local], rows_ref[0:1, pair_local : 2 * pair_local]
    )


def part_widths(cols):
    unit = cols // (128 * sum(part_tiles)) * 128
    if unit == 0 or unit * sum(part_tiles) != cols:
        return (cols,)
    return tuple(unit * tile for tile in part_tiles)


def paired_local(hidden, head_weight, targets, response_mask, labels, reference_sums):
    return paired_body(
        hidden, head_weight, targets, response_mask, labels, reference_sums
    )


def paired_body(hidden, head_weight, targets, response_mask, labels, reference_sums):
    rows = hidden.shape[0]
    depth, cols = head_weight.shape
    pair_local = labels.shape[0]
    pair_total = 2 * pair_local
    span = rows // (2 * pair_local)
    count = lax.axis_size("vocab")
    half = count // 2
    plane = lax.axis_index("tok")
    spot = lax.axis_index("vocab")
    moves = spot // half != plane

    where = jnp.stack([spot, plane, jnp.full_like(spot, half)]).astype(jnp.int32)
    info = jnp.concatenate(
        [
            targets.astype(jnp.float32)[None],
            response_mask.astype(jnp.float32)[None],
            jnp.pad(labels.astype(jnp.float32)[None], ((0, 0), (0, rows - pair_local))),
            jnp.pad(reference_sums.T, ((0, 0), (0, rows - pair_local))),
            jnp.zeros((3, rows), jnp.float32),
        ],
        axis=0,
    )
    where, moves, info, head_weight = lax.optimization_barrier((where, moves, info, head_weight))
    piece = plane_swap(hidden.T, count, moves)
    head_weight = load(head_weight)
    hidden_t, hidden_n = gather_hidden(piece, where, count)
    rows_info, local_targets = small_call(
        functools.partial(side_kernel, cols),
        [((8, 2 * rows), jnp.float32), ((2 * rows, 1), jnp.int32)],
        [where, info, over(info)],
    )
    picked = pick(where, local_targets, head_weight, count)

    scale = 1.0
    while hidden_bound * weight_bound * depth * scale > half_limit:
        scale *= 0.5
    widths = part_widths(cols)
    starts = [sum(widths[:part]) for part in range(len(widths))]
    swapped = []
    for start, width in zip(starts, widths):
        own = logit_part(start, width, hidden_n, head_weight)
        sent = (own * scale if scale != 1.0 else own).astype(jnp.float16)
        got = over(sent)
        swapped.append((own, got))
    logit_parts = []
    state = None
    for part, (start, width) in enumerate(zip(starts, widths)):
        own, got = swapped[part]
        got = got.astype(jnp.float32)
        logits = own + (got * (1.0 / scale) if scale != 1.0 else got)
        logit_parts.append(logits)
        state = fold(start, width, logits, local_targets, head_weight, state)
    stats, grad = state
    hidden_part, row_values, margin_rows = finish(
        grad, stats, picked, rows_info, where, count, span, pair_total
    )
    hidden_got = plane_swap(hidden_part, count, None)
    other_rows = over(margin_rows)
    logits = jnp.concatenate(logit_parts, axis=1)
    head_grad = head_blocks(hidden_t, logits, row_values, local_targets)
    hidden_grad_t, mean_loss, margins = small_call(
        functools.partial(last_kernel, pair_local),
        [(hidden_part.shape, hidden.dtype), ((1, 1), jnp.float32), ((1, pair_local), jnp.float32)],
        [where, margin_rows, other_rows, hidden_part, hidden_got],
    )
    hidden_grad = hidden_grad_t.T
    mean_loss, margins = mean_loss.reshape(()), margins.reshape(pair_local)
    return (mean_loss, margins, hidden_grad, head_grad)


def solution(mesh):
    count = mesh.shape["vocab"]
    paired = mesh.shape["tok"] == 2 and count == 16
    return jax.shard_map(
        paired_local if paired else general_local,
        mesh=mesh,
        in_specs=(
            P("tok", "vocab"),
            P("tok", "vocab"),
            P("tok"),
            P("tok"),
            P("tok"),
            P("tok", None),
        ),
        out_specs=(P(), P("tok"), P("tok", "vocab"), P("tok", "vocab")),
        check_vma=False,
    )
```

```python
import functools
import math

import jax
import jax.numpy as jnp
from jax import lax
from jax.experimental import pallas as pl
from jax.experimental.pallas import tpu as pltpu
from jax.sharding import PartitionSpec as P


beta_scale = 0.1
tie_offset = math.log(2.0)
tie_const = math.log(3.0)
grad_scale = 512.0


def pair_terms(margins, labels):
    winner = labels.astype(jnp.float32)
    log_tie = (
        tie_const
        + margins
        - tie_offset
        - jax.nn.softplus(margins - tie_offset)
        - jax.nn.softplus(margins + tie_offset)
    )
    losses = winner * jax.nn.softplus(tie_offset - margins) - (1.0 - winner) * log_tie
    slopes = -winner * jax.nn.sigmoid(tie_offset - margins) - (1.0 - winner) * (
        1.0 - jax.nn.sigmoid(margins - tie_offset) - jax.nn.sigmoid(margins + tie_offset)
    )
    return (losses, slopes)


def add_parts(received):
    return jnp.sum(received, axis=0)


def general_local(hidden, head_weight, targets, response_mask, labels, reference_sums):
    tok_rows = hidden.shape[0]
    vocab_cols = head_weight.shape[1]
    tok_count = lax.axis_size("tok")
    pair_local = labels.shape[0]
    pair_total = pair_local * tok_count
    span = tok_rows // (2 * pair_local)
    rows_full = lax.all_gather(hidden, "vocab", axis=1, tiled=True)
    token_cols = lax.all_to_all(rows_full, "tok", split_axis=1, concat_axis=0, tiled=True)
    partial_value = jnp.dot(token_cols, head_weight, preferred_element_type=jnp.float32)
    partial_value = partial_value.reshape(tok_count, tok_rows, vocab_cols)
    logits = add_parts(
        lax.all_to_all(partial_value, "tok", split_axis=0, concat_axis=0, tiled=True)
    )
    offset = lax.axis_index("vocab") * vocab_cols
    columns = lax.broadcasted_iota(jnp.int32, (1, vocab_cols), 1) + offset
    matched = columns == targets[:, None]
    local_max = jnp.max(logits, axis=1)
    local_target = jnp.sum(jnp.where(matched, logits, 0.0), axis=1)
    row_max = lax.pmax(local_max, "vocab")
    shifted = jnp.exp(logits - row_max[:, None])
    totals, target_logit = lax.psum((jnp.sum(shifted, axis=1), local_target), "vocab")
    probs = shifted / totals[:, None]
    token_logp = target_logit - (row_max + jnp.log(totals))
    weights = response_mask.astype(jnp.float32)
    sequence_logp = jnp.sum((token_logp * weights).reshape(pair_local, 2, span), axis=2)
    ratios = sequence_logp - reference_sums
    margins = beta_scale * (ratios[:, 0] - ratios[:, 1])
    losses, slopes = pair_terms(margins, labels)
    mean_loss = lax.psum(jnp.sum(losses), "tok") / pair_total
    pair_coef = beta_scale * grad_scale / pair_total * slopes
    signed = jnp.stack([pair_coef, -pair_coef], axis=1)
    token_coef = (
        jnp.broadcast_to(signed[:, :, None], (pair_local, 2, span)).reshape(tok_rows) * weights
    )
    onehot = jnp.where(matched, 1.0, 0.0).astype(jnp.float32)
    dlogits = (token_coef[:, None] * (onehot - probs)).astype(jnp.bfloat16)
    dlogit_all = lax.all_gather(dlogits, "tok", axis=0, tiled=True)
    head_grad = lax.dot_general(
        token_cols, dlogit_all, (((0,), (0,)), ((), ())), preferred_element_type=jnp.float32
    ).astype(jnp.bfloat16)
    partial_grad = lax.dot_general(
        head_weight, dlogit_all, (((1,), (1,)), ((), ())), preferred_element_type=jnp.float32
    )
    returned = lax.all_to_all(
        partial_grad.astype(jnp.bfloat16), "tok", split_axis=1, concat_axis=0, tiled=True
    ).astype(partial_grad.dtype)
    grad_cols = lax.psum_scatter(returned, "vocab", scatter_dimension=0, tiled=True)
    hidden_grad = grad_cols.T.astype(jnp.bfloat16)
    return (mean_loss, margins, hidden_grad, head_grad)


swap_pairs = ((0, 1), (1, 0))
hidden_bound = 8.0
weight_bound = 4.0
half_limit = 60000.0
part_tiles = (2, 4, 8, 8, 8, 6, 2, 2)
mebi = 1 << 20
stats_rows = 16


def exclusive(count, mask):
    return [(spot, spot ^ mask) for spot in range(count)]


def across(value, count, mask):
    return lax.ppermute(value, "vocab", exclusive(count, mask))


def over(value):
    return lax.ppermute(value, "tok", swap_pairs)


def plane_swap(value, count, moves):
    half = count // 2
    pairs = []
    for plane in range(2):
        for spot in range(count):
            if spot // half != plane:
                pairs.append((2 * spot + plane, 2 * (spot ^ half) + 1 - plane))
    received = lax.ppermute(value, ("vocab", "tok"), pairs)
    return received if moves is None else jnp.where(moves, received, value)


def place_kernel(order, spot_ref, *refs):
    hidden_t_ref, hidden_n_ref = refs[-2:]
    slots, feats, rows = refs[0].shape
    half = 2 * slots
    spot = spot_ref[0]
    for side, ref in zip((0, 2, 1, 3), refs[:-2]):
        for slot in range(slots):
            source = spot ^ (order[slot] ^ side)
            start = pl.multiple_of((source % half) * feats, 32)
            column = pl.multiple_of((source // half) * rows, 128)
            hidden_t_ref[pl.ds(start, feats), pl.ds(column, rows)] = ref[slot]
    depth = hidden_t_ref.shape[0]
    step = 256 if depth % 256 == 0 else 128
    for start in range(0, depth, step):
        hidden_n_ref[:, start : start + step] = hidden_t_ref[start : start + step, :].T


def fold_kernel(start, has_state, logits_ref, target_ref, upper_ref, lower_ref, *refs):
    if has_state:
        stats_ref, grad_ref, new_stats_ref, new_grad_ref, terms_ref = refs
    else:
        new_stats_ref, new_grad_ref, terms_ref = refs
    logits = logits_ref[...]
    width = logits.shape[1]
    columns = lax.broadcasted_iota(jnp.int32, logits.shape, 1) + start
    hit = columns == target_ref[...]
    top = jnp.max(logits, axis=1, keepdims=True)
    if has_state:
        old = stats_ref[...].T
        old_top = old[:, 0:1]
        top = jnp.maximum(top, old_top)
    terms = jnp.exp(logits - top)
    total = jnp.sum(terms, axis=1, keepdims=True)
    target = jnp.sum(jnp.where(hit, logits, 0.0), axis=1, keepdims=True)
    terms_ref[...] = jnp.where(hit, 0.0, terms).astype(jnp.bfloat16)
    shrink = jnp.ones_like(top)
    if has_state:
        shrink = jnp.exp(old_top - top)
        total = total + old[:, 1:2] * shrink
        target = target + old[:, 2:3]
    lane = lax.broadcasted_iota(jnp.int32, (logits.shape[0], 128), 1)
    packed = jnp.where(
        lane == 0, top, jnp.where(lane == 1, total, jnp.where(lane == 2, target, shrink))
    ).T
    new_stats_ref[...] = packed[0:8]
    shrink_row = packed[3:4]
    step = upper_ref.shape[0]
    for first, weight_ref in ((0, upper_ref), (step, lower_ref)):
        part = lax.dot_general(
            weight_ref[:, start : start + width],
            terms_ref[...],
            (((1,), (1,)), ((), ())),
            preferred_element_type=jnp.float32,
        )
        if has_state:
            part = part + grad_ref[first : first + step, :] * shrink_row
        new_grad_ref[first : first + step, :] = part


def fold(start, width, logits, local_targets, head_weight, state):
    tokens = logits.shape[0]
    depth = 2 * head_weight[0].shape[0]
    args = [logits, local_targets, *head_weight]
    aliases = {}
    if state is not None:
        args += list(state)
        aliases = {5: 1}
    return pl.pallas_call(
        functools.partial(fold_kernel, start, state is not None),
        out_shape=(
            jax.ShapeDtypeStruct((8, tokens), jnp.float32),
            jax.ShapeDtypeStruct((depth, tokens), jnp.float32),
        ),
        in_specs=vmem_specs(len(args)),
        out_specs=tuple(vmem_specs(2)),
        scratch_shapes=[pltpu.VMEM((tokens, width), jnp.bfloat16)],
        input_output_aliases=aliases,
        compiler_params=pltpu.CompilerParams(vmem_limit_bytes=12 * mebi),
        cost_estimate=pl.CostEstimate(
            flops=2 * depth * tokens * width,
            transcendentals=tokens * width,
            bytes_accessed=2 * depth * width + 4 * tokens * width + 8 * depth * tokens,
        ),
    )(*args)


def load_kernel(first, source_ref, held_ref, sems):
    number = sems.shape[0]
    rows = held_ref.shape[0] // number
    copies = [
        pltpu.make_async_copy(
            source_ref.at[pl.ds(first + index * rows, rows)],
            held_ref.at[pl.ds(index * rows, rows)],
            sems.at[index],
        )
        for index in range(number)
    ]
    for copy in copies:
        copy.start()
    for copy in copies:
        copy.wait()


def load(head_weight, first, rows, limit):
    cols = head_weight.shape[1]
    number = 4 if rows % 64 == 0 else 1
    return pl.pallas_call(
        functools.partial(load_kernel, first),
        out_shape=pltpu.VMEM((rows, cols), head_weight.dtype),
        in_specs=[pl.BlockSpec(memory_space=pl.ANY)],
        out_specs=pl.BlockSpec(memory_space=pltpu.VMEM),
        scratch_shapes=[pltpu.SemaphoreType.DMA((number,))],
        compiler_params=pltpu.CompilerParams(vmem_limit_bytes=limit * mebi),
        cost_estimate=pl.CostEstimate(flops=0, transcendentals=0, bytes_accessed=2 * rows * cols),
    )(head_weight)


def logit_kernel(start, hidden_ref, upper_ref, lower_ref, out_ref):
    width = out_ref.shape[1]
    half = upper_ref.shape[0]
    step = 256 if width % 256 == 0 else width
    for first in range(0, width, step):
        out_ref[:, first : first + step] = jnp.dot(
            hidden_ref[:, :half],
            upper_ref[:, start + first : start + first + step],
            preferred_element_type=jnp.float32,
        ) + jnp.dot(
            hidden_ref[:, half:],
            lower_ref[:, start + first : start + first + step],
            preferred_element_type=jnp.float32,
        )


def logit_part(start, width, hidden_n, head_weight):
    tokens, depth = hidden_n.shape
    return pl.pallas_call(
        functools.partial(logit_kernel, start),
        out_shape=jax.ShapeDtypeStruct((tokens, width), jnp.float32),
        in_specs=vmem_specs(3),
        out_specs=vmem_specs(1)[0],
        compiler_params=pltpu.CompilerParams(vmem_limit_bytes=12 * mebi),
        cost_estimate=pl.CostEstimate(
            flops=2 * depth * tokens * width, transcendentals=0, bytes_accessed=2 * depth * width
        ),
    )(hidden_n, *head_weight)


def gather_hidden(piece, where, count):
    order = [0]
    parts = [piece]
    for mask in range(4, count, 4):
        order.append(mask)
        parts.append(across(piece, count, mask))
    feats, rows = piece.shape
    stacked = jnp.concatenate(parts, axis=0)
    side = across(stacked, count, 2)
    groups = [stacked, side, across(stacked, count, 1), across(side, count, 1)]
    slots = len(order)
    depth = 2 * slots * feats
    return pl.pallas_call(
        lambda *refs: place_kernel(order, *refs),
        out_shape=(
            jax.ShapeDtypeStruct((depth, 2 * rows), piece.dtype),
            jax.ShapeDtypeStruct((2 * rows, depth), piece.dtype),
        ),
        in_specs=[pl.BlockSpec(memory_space=pltpu.SMEM)]
        + [pl.BlockSpec(memory_space=pltpu.VMEM)] * len(groups),
        out_specs=[pl.BlockSpec(memory_space=pltpu.VMEM)] * 2,
        compiler_params=pltpu.CompilerParams(vmem_limit_bytes=8 * mebi),
        cost_estimate=pl.CostEstimate(flops=0, transcendentals=0, bytes_accessed=4000000),
    )(
        where,
        *[group.reshape(slots, feats, rows) for group in groups],
    )


def pick_kernel(feats, spot_ref, target_ref, upper_ref, lower_ref, keep_ref, send_ref, sum_ref):
    half, cols = upper_ref.shape
    width = 1024 if cols % 1024 == 0 else cols
    columns = lax.broadcasted_iota(jnp.int32, (target_ref.shape[0], width), 1)
    for start in range(0, cols, width):
        hit = columns + start == target_ref[...]
        ones = jnp.where(hit, 1.0, 0.0).astype(jnp.bfloat16)
        for first, weight_ref in ((0, upper_ref), (half, lower_ref)):
            part = lax.dot_general(
                weight_ref[:, start : start + width],
                ones,
                (((1,), (1,)), ((), ())),
                preferred_element_type=jnp.float32,
            )
            if start == 0:
                sum_ref[first : first + half, :] = part
            else:
                sum_ref[first : first + half, :] += part
    bit = spot_ref[0] % 2
    for group in range(keep_ref.shape[0] // feats):
        out = pl.ds(group * feats, feats)
        near = pl.multiple_of((2 * group + bit) * feats, 8)
        far = pl.multiple_of((2 * group + 1 - bit) * feats, 8)
        keep_ref[out, :] = sum_ref[pl.ds(near, feats), :].astype(jnp.bfloat16)
        send_ref[out, :] = sum_ref[pl.ds(far, feats), :].astype(jnp.bfloat16)


def pick_next_kernel(feats, spot_ref, old_ref, got_ref, keep_ref, send_ref):
    def value(group):
        rows = pl.ds(pl.multiple_of(group * feats, 16), feats)
        return old_ref[rows, :] + got_ref[rows, :]

    bit = (spot_ref[0] // 2) % 2
    for group in range(keep_ref.shape[0] // feats):
        out = pl.ds(group * feats, feats)
        keep_ref[out, :] = value(2 * group + bit)
        send_ref[out, :] = value(2 * group + 1 - bit)


def pick_spread_kernel(feats, spot_ref, old_ref, got_ref, *outs):
    place = spot_ref[0] // 4
    rows = outs[0].shape[1]
    for shift in range(4):
        chosen = place ^ shift
        group = pl.ds(pl.multiple_of((chosen % 2) * feats, 16), feats)
        value = old_ref[group, :].astype(jnp.float32) + got_ref[group, :].astype(jnp.float32)
        value = jnp.where(chosen // 2 == 0, value[:, :rows], value[:, rows:])
        outs[shift][...] = value.astype(jnp.bfloat16)


def pick(where, local_targets, head_weight, count):
    tokens = local_targets.shape[0]
    depth, cols = 2 * head_weight[0].shape[0], head_weight[0].shape[1]
    feats = 2 * depth // count
    rows = tokens // 2
    bf16 = jnp.bfloat16
    keep, send = pl.pallas_call(
        functools.partial(pick_kernel, feats),
        out_shape=[jax.ShapeDtypeStruct((depth // 2, tokens), bf16)] * 2,
        in_specs=[pl.BlockSpec(memory_space=pltpu.SMEM)] + vmem_specs(3),
        out_specs=vmem_specs(2),
        scratch_shapes=[pltpu.VMEM((depth, tokens), jnp.float32)],
        compiler_params=pltpu.CompilerParams(vmem_limit_bytes=14 * mebi),
        cost_estimate=pl.CostEstimate(
            flops=2 * depth * tokens * cols,
            transcendentals=0,
            bytes_accessed=2 * depth * cols,
        ),
    )(where, local_targets, *head_weight)
    got = across(send, count, 1)
    keep, send = small_call(
        functools.partial(pick_next_kernel, feats),
        [((depth // 4, tokens), bf16)] * 2,
        [where, keep, got],
    )
    got = across(send, count, 2)
    keep, *sends = small_call(
        functools.partial(pick_spread_kernel, feats),
        [((feats, rows), bf16)] * 4,
        [where, keep, got],
    )
    return [keep] + [across(send, count, 4 * shift) for shift, send in zip((1, 2, 3), sends)]


def side_kernel(cols, place_ref, own_ref, other_ref, rows_ref, target_ref):
    swap = place_ref[1] != 0
    own, other = own_ref[...], other_ref[...]
    both = jnp.concatenate(
        [jnp.where(swap, other, own), jnp.where(swap, own, other)], axis=1
    )
    rows_ref[...] = both
    target_ref[...] = both.T[:, 0:1].astype(jnp.int32) - place_ref[0] * cols


def vmem_specs(number):
    return [pl.BlockSpec(memory_space=pltpu.VMEM)] * number


def put_stats(ref, start, rows):
    rows = rows[0:3]
    high = rows.astype(jnp.bfloat16).astype(jnp.float32)
    rest = rows - high
    middle = rest.astype(jnp.bfloat16).astype(jnp.float32)
    blank = jnp.zeros((stats_rows - 9, rows.shape[1]), jnp.float32)
    block = jnp.concatenate([high, middle, rest - middle, blank], axis=0)
    ref[start : start + stats_rows, :] = block.astype(jnp.bfloat16)


def get_stats(ref, start):
    block = ref[start : start + stats_rows, :].astype(jnp.float32)
    blank = jnp.zeros((5, block.shape[1]), jnp.float32)
    return jnp.concatenate([block[0:3] + block[3:6] + block[6:9], blank], axis=0)


def merged_rows(bit, own, other):
    swap = bit != 0
    first = jnp.where(swap, other, own)
    second = jnp.where(swap, own, other)
    top = jnp.maximum(first[0:1], second[0:1])
    total = first[1:2] * jnp.exp(first[0:1] - top) + second[1:2] * jnp.exp(second[0:1] - top)
    target = first[2:3] + second[2:3]
    return jnp.concatenate([top, total, target, jnp.zeros((5, own.shape[1]), own.dtype)], axis=0)


def first_half_kernel(feats, spot_ref, grad_ref, stats_ref, keep_ref, send_ref):
    bit = spot_ref[0] % 2
    groups = keep_ref.shape[0] // feats
    for group in range(groups):
        out = pl.ds(group * feats, feats)
        near = pl.multiple_of((2 * group + bit) * feats, 8)
        far = pl.multiple_of((2 * group + 1 - bit) * feats, 8)
        keep_ref[out, :] = grad_ref[pl.ds(near, feats), :]
        send_ref[out, :] = grad_ref[pl.ds(far, feats), :].astype(jnp.bfloat16)
    put_stats(send_ref, groups * feats, stats_ref[...])


def halved(old_ref, got_ref, stats_ref, bit):
    own = stats_ref[...]
    other = get_stats(got_ref, old_ref.shape[0])
    merged = merged_rows(bit, own, other)
    return merged, jnp.exp(own[0:1] - merged[0:1]), jnp.exp(other[0:1] - merged[0:1])


def next_half_kernel(
    feats, mask, spot_ref, old_ref, got_ref, stats_ref, keep_ref, send_ref, new_stats_ref
):
    spot = spot_ref[0]
    merged, own_factor, other_factor = halved(old_ref, got_ref, stats_ref, (spot // mask) % 2)

    def value(group):
        rows = pl.ds(pl.multiple_of(group * feats, 16), feats)
        return old_ref[rows, :] * own_factor + got_ref[rows, :].astype(jnp.float32) * other_factor

    bit = (spot // (2 * mask)) % 2
    groups = keep_ref.shape[0] // feats
    for group in range(groups):
        out = pl.ds(group * feats, feats)
        keep_ref[out, :] = value(2 * group + bit)
        send_ref[out, :] = value(2 * group + 1 - bit).astype(jnp.bfloat16)
    put_stats(send_ref, groups * feats, merged)
    new_stats_ref[...] = merged


def spread_kernel(feats, spot_ref, old_ref, got_ref, stats_ref, keep_ref, new_stats_ref, *sends):
    spot = spot_ref[0]
    merged, own_factor, other_factor = halved(old_ref, got_ref, stats_ref, (spot // 2) % 2)
    new_stats_ref[...] = merged
    place = spot // 4
    rows = keep_ref.shape[1]
    for shift in range(4):
        chosen = place ^ shift
        group = pl.ds(pl.multiple_of((chosen % 2) * feats, 16), feats)
        left = chosen // 2 == 0
        value = old_ref[group, :] * own_factor + got_ref[group, :].astype(jnp.float32) * other_factor
        value = jnp.where(left, value[:, :rows], value[:, rows:])
        if shift == 0:
            keep_ref[...] = value
        else:
            send_ref = sends[shift - 1]
            send_ref[0:feats, :] = value.astype(jnp.bfloat16)
            put_stats(send_ref, feats, merged[:, :rows])
            put_stats(send_ref, feats + stats_rows, merged[:, rows:])


def finish_kernel(
    span,
    pair_total,
    spot_ref,
    keep_ref,
    one_ref,
    two_ref,
    three_ref,
    stats_ref,
    picked_a_ref,
    picked_b_ref,
    picked_c_ref,
    picked_d_ref,
    rows_ref,
    grad_ref,
    columns_ref,
    margins_ref,
):
    feats, rows = keep_ref.shape
    place = spot_ref[0] // 4
    sent = [one_ref, two_ref, three_ref]
    quads = [stats_ref[...]] + [
        jnp.concatenate([get_stats(ref, feats), get_stats(ref, feats + stats_rows)], axis=1) for ref in sent
    ]
    low = place % 2
    pair_one = merged_rows(low, quads[0], quads[1])
    pair_two = merged_rows(low, quads[2], quads[3])
    final = merged_rows(place // 2, pair_one, pair_two)
    top, total, target = final[0:1], final[1:2], final[2:3]
    weights = rows_ref[1:2, :]
    pair_local = pair_total // 2
    scored = (target - (top + jnp.log(total))) * weights
    sequence = lax.broadcasted_iota(jnp.int32, scored.shape, 1) // span
    lane = lax.broadcasted_iota(jnp.int32, (8, 128), 1)
    coef = jnp.zeros_like(scored)
    margins_out = losses_out = jnp.zeros(lane.shape, jnp.float32)

    def lane_of(pair):
        place = (pair // pair_local) * rows + pair % pair_local
        return slice(place, place + 1)

    for pair in range(pair_total):
        sums = [
            jnp.sum(jnp.where(sequence == 2 * pair + side, scored, 0.0), axis=1, keepdims=True)
            - rows_ref[3 + side : 4 + side, lane_of(pair)]
            for side in range(2)
        ]
        margin = beta_scale * (sums[0] - sums[1])
        winner = rows_ref[2:3, lane_of(pair)]
        loss, slope = pair_terms(margin, winner)
        scaled = beta_scale * grad_scale / pair_total * slope
        coef = jnp.where(sequence == 2 * pair, scaled, coef)
        coef = jnp.where(sequence == 2 * pair + 1, -scaled, coef)
        margins_out = jnp.where(lane == pair, margin, margins_out)
        losses_out = jnp.where(lane == pair, loss, losses_out)
    coef = coef * weights
    margins_ref[0:8, :] = margins_out
    margins_ref[8:16, :] = losses_out
    inverse = 1.0 / total
    blank = jnp.zeros((5, coef.shape[1]), jnp.float32)
    columns_ref[...] = jnp.concatenate([coef, top, inverse, blank], axis=0).T

    left = place // 2 == 0

    def own_block(row):
        return jnp.where(left, row[:, :rows], row[:, rows:])

    value = keep_ref[...] * own_block(jnp.exp(quads[0][0:1] - top))
    for ref, quad in zip(sent, quads[1:]):
        value = value + ref[0:feats, :].astype(jnp.float32) * own_block(jnp.exp(quad[0:1] - top))
    picked = sum(
        ref[...].astype(jnp.float32)
        for ref in (picked_a_ref, picked_b_ref, picked_c_ref, picked_d_ref)
    )
    picked_coef = coef * (1.0 - jnp.exp(target - top) * inverse)
    grad_ref[...] = (
        own_block(picked_coef) * picked
        - own_block(coef * inverse) * value
    ).astype(jnp.bfloat16)


def small_call(kernel, outs, args):
    return pl.pallas_call(
        kernel,
        out_shape=[jax.ShapeDtypeStruct(shape, dtype) for shape, dtype in outs],
        in_specs=[pl.BlockSpec(memory_space=pltpu.SMEM)] + vmem_specs(len(args) - 1),
        out_specs=vmem_specs(len(outs)),
        compiler_params=pltpu.CompilerParams(vmem_limit_bytes=12 * mebi),
        cost_estimate=pl.CostEstimate(flops=0, transcendentals=0, bytes_accessed=2000000),
    )(*args)


def finish(grad, stats, picked, rows_info, where, count, span, pair_total):
    depth, tokens = grad.shape
    feats = 2 * depth // count
    rows = tokens // 2
    f32, bf16 = jnp.float32, jnp.bfloat16
    half, quarter = depth // 2, depth // 4
    keep, send = small_call(
        functools.partial(first_half_kernel, feats),
        [((half, tokens), f32), ((half + stats_rows, tokens), bf16)],
        [where, grad, stats],
    )
    got = across(send, count, 1)
    keep, send, stats = small_call(
        functools.partial(next_half_kernel, feats, 1),
        [((quarter, tokens), f32), ((quarter + stats_rows, tokens), bf16), ((8, tokens), f32)],
        [where, keep, got, stats],
    )
    got = across(send, count, 2)
    keep, stats, *sends = small_call(
        functools.partial(spread_kernel, feats),
        [((feats, rows), f32), ((8, tokens), f32)] + [((feats + 2 * stats_rows, rows), bf16)] * 3,
        [where, keep, got, stats],
    )
    gots = [across(send, count, 4 * shift) for shift, send in zip((1, 2, 3), sends)]
    return small_call(
        functools.partial(finish_kernel, span, pair_total),
        [((feats, rows), bf16), ((tokens, 8), f32), ((16, 128), f32)],
        [where, keep, *gots, stats, *picked, rows_info],
    )


def head_kernel(hidden_ref, logits_ref, rows_ref, target_ref, out_ref):
    width = out_ref.shape[1]
    coef, top, inverse = rows_ref[:, 0:1], rows_ref[:, 1:2], rows_ref[:, 2:3]
    depth = out_ref.shape[0]
    rows = 256 if depth % 256 == 0 else depth
    part = 256 if width % 256 == 0 else width
    columns = lax.broadcasted_iota(jnp.int32, (logits_ref.shape[0], part), 1)
    start = pl.program_id(0) * width
    for column in range(0, width, part):
        onehot = jnp.where(columns + (start + column) == target_ref[...], 1.0, 0.0)
        probs = jnp.exp(logits_ref[:, column : column + part] - top) * inverse
        dlogits = (coef * (onehot - probs)).astype(jnp.bfloat16)
        for first in range(0, depth, rows):
            out_ref[first : first + rows, column : column + part] = jnp.dot(
                hidden_ref[first : first + rows, :],
                dlogits,
                preferred_element_type=jnp.float32,
            ).astype(out_ref.dtype)


def head_blocks(hidden_t, logits, row_values, local_targets):
    depth, tokens = hidden_t.shape
    cols = logits.shape[1]
    width = cols // 4 if cols % (4 * 256) == 0 else cols
    whole = lambda step: (0, 0)
    column = lambda step: (0, step)
    return pl.pallas_call(
        head_kernel,
        out_shape=jax.ShapeDtypeStruct((depth, cols), jnp.bfloat16),
        grid=(cols // width,),
        in_specs=[
            pl.BlockSpec((depth, tokens), whole),
            pl.BlockSpec((tokens, width), column),
            pl.BlockSpec((tokens, 8), whole),
            pl.BlockSpec((tokens, 1), whole),
        ],
        out_specs=pl.BlockSpec((depth, width), column),
        compiler_params=pltpu.CompilerParams(vmem_limit_bytes=40 * mebi),
        cost_estimate=pl.CostEstimate(
            flops=2 * depth * tokens * cols,
            transcendentals=tokens * cols,
            bytes_accessed=(2 * depth + 4 * tokens) * cols,
        ),
    )(hidden_t, logits, row_values, local_targets)


def last_kernel(pair_local, place_ref, rows_ref, other_ref, own_ref, got_ref, grad_ref, loss_ref, margin_ref):
    half = place_ref[2]
    plane = place_ref[1]
    first = plane == 0
    moved = jnp.where(
        place_ref[0] // half != plane,
        got_ref[...].astype(jnp.float32),
        own_ref[...].astype(jnp.float32),
    )
    grad_ref[...] = moved.astype(grad_ref.dtype)
    total = jnp.zeros((1, 1), jnp.float32)
    for pair in range(2 * pair_local):
        own, other = rows_ref[8:9, pair : pair + 1], other_ref[8:9, pair : pair + 1]
        total = total + jnp.where(first == (pair < pair_local), own, other)
    loss_ref[...] = total / (2 * pair_local)
    margin_ref[...] = jnp.where(
        first, rows_ref[0:1, 0:pair_local], rows_ref[0:1, pair_local : 2 * pair_local]
    )


def part_widths(cols):
    unit = cols // (128 * sum(part_tiles)) * 128
    if unit == 0 or unit * sum(part_tiles) != cols:
        return (cols,)
    return tuple(unit * tile for tile in part_tiles)


def paired_local(hidden, head_weight, targets, response_mask, labels, reference_sums):
    return paired_body(
        hidden, head_weight, targets, response_mask, labels, reference_sums
    )


def paired_body(hidden, head_weight, targets, response_mask, labels, reference_sums):
    rows = hidden.shape[0]
    depth, cols = head_weight.shape
    pair_local = labels.shape[0]
    pair_total = 2 * pair_local
    span = rows // (2 * pair_local)
    count = lax.axis_size("vocab")
    half = count // 2
    plane = lax.axis_index("tok")
    spot = lax.axis_index("vocab")
    moves = spot // half != plane

    where = jnp.stack([spot, plane, jnp.full_like(spot, half)]).astype(jnp.int32)
    info = jnp.concatenate(
        [
            targets.astype(jnp.float32)[None],
            response_mask.astype(jnp.float32)[None],
            jnp.pad(labels.astype(jnp.float32)[None], ((0, 0), (0, rows - pair_local))),
            jnp.pad(reference_sums.T, ((0, 0), (0, rows - pair_local))),
            jnp.zeros((3, rows), jnp.float32),
        ],
        axis=0,
    )
    where, moves, info, head_weight = lax.optimization_barrier((where, moves, info, head_weight))
    piece = plane_swap(hidden.T, count, moves)
    upper = load(head_weight, 0, depth // 2, 48)
    lower = load(head_weight, depth // 2, depth // 2, 40)
    head_weight = (upper, lower)
    hidden_t, hidden_n = gather_hidden(piece, where, count)
    rows_info, local_targets = small_call(
        functools.partial(side_kernel, cols),
        [((8, 2 * rows), jnp.float32), ((2 * rows, 1), jnp.int32)],
        [where, info, over(info)],
    )
    picked = pick(where, local_targets, head_weight, count)

    scale = 1.0
    while hidden_bound * weight_bound * depth * scale > half_limit:
        scale *= 0.5
    widths = part_widths(cols)
    starts = [sum(widths[:part]) for part in range(len(widths))]
    swapped = []
    for start, width in zip(starts, widths):
        own = logit_part(start, width, hidden_n, head_weight)
        sent = (own * scale if scale != 1.0 else own).astype(jnp.float16)
        got = over(sent)
        swapped.append((own, got))
    logit_parts = []
    state = None
    for part, (start, width) in enumerate(zip(starts, widths)):
        own, got = swapped[part]
        got = got.astype(jnp.float32)
        logits = own + (got * (1.0 / scale) if scale != 1.0 else got)
        logit_parts.append(logits)
        state = fold(start, width, logits, local_targets, head_weight, state)
    stats, grad = state
    hidden_part, row_values, margin_rows = finish(
        grad, stats, picked, rows_info, where, count, span, pair_total
    )
    hidden_got = plane_swap(hidden_part, count, None)
    other_rows = over(margin_rows)
    logits = jnp.concatenate(logit_parts, axis=1)
    head_grad = head_blocks(hidden_t, logits, row_values, local_targets)
    hidden_grad_t, mean_loss, margins = small_call(
        functools.partial(last_kernel, pair_local),
        [(hidden_part.shape, hidden.dtype), ((1, 1), jnp.float32), ((1, pair_local), jnp.float32)],
        [where, margin_rows, other_rows, hidden_part, hidden_got],
    )
    hidden_grad = hidden_grad_t.T
    mean_loss, margins = mean_loss.reshape(()), margins.reshape(pair_local)
    return (mean_loss, margins, hidden_grad, head_grad)


def solution(mesh):
    count = mesh.shape["vocab"]
    paired = mesh.shape["tok"] == 2 and count == 16
    return jax.shard_map(
        paired_local if paired else general_local,
        mesh=mesh,
        in_specs=(
            P("tok", "vocab"),
            P("tok", "vocab"),
            P("tok"),
            P("tok"),
            P("tok"),
            P("tok", None),
        ),
        out_specs=(P(), P("tok"), P("tok", "vocab"), P("tok", "vocab")),
        check_vma=False,
    )
```
